512 devices in a mesh: expert: 64 (over x, z), dp: 4 (over y), pair: 2 (over core).
Axes of the slice: x: 4, y: 4, z: 16, core: 2. Of those that a mesh axis runs over, the one named last changes fastest.
Arguments:
- byte_states: bfloat16 [65536, 2048], P(('expert', 'dp')), may hold values from -6 to 6
- positions: int32 [32768], P(('expert', 'dp')), may hold values from 0 to 65535, as said below
- picks: int32 [32768, 2], P(('expert', 'dp')), may hold values from 0 to 63, all different within a row; in each aligned block of 128 rows (0 to 127, 128 to 255, ...) at most 5 rows name the same one
- cotangent: bfloat16 [32768, 2048], P(('expert', 'dp')), may hold values from -6 to 6
- router_weight: bfloat16 [2048, 64], replicated, may hold values from -0.125 to 0.125
- gate_weight: bfloat16 [64, 2048, 768], P('expert', 'dp', 'pair'), may hold values from -0.125 to 0.125
- up_weight: bfloat16 [64, 2048, 768], P('expert', 'dp', 'pair'), may hold values from -0.125 to 0.125
- down_weight: bfloat16 [64, 2048, 768], P('expert', 'dp', 'pair'), may hold values from -0.21875 to 0.21875
Outputs:
- row_grad: bfloat16 [32768, 2048], P(('expert', 'dp'))
- gate_grad: bfloat16 [64, 2048, 768], P('expert', 'dp', 'pair')
- up_grad: bfloat16 [64, 2048, 768], P('expert', 'dp', 'pair')
The draws below stay inside these ranges and needn't reach their ends.
Inputs may be any that keep to these rules, and one draw needn't show every extreme that they name: `positions`: Increasing; the j-th block of 128 rows points into the bytes j * 256 to (j + 1) * 256 - 1 and names the first and the last of them. The 2 picks of a row differ; in each aligned block of 128 rows (the rows of one index of expert and dp) no expert is named by more than 5 rows, a bound that some block reaches.
All inputs are finite; a program needn't handle non-finite values.
Results may differ from the reference program's by a relative error of at most 0.011.
Values may be sent and summed in bfloat16 or wider, within the bound.
No kernel may reach another device: no remote copies, remote signals or barrier semaphores. Data moves between devices by JAX's collectives and lax.ppermute only.
A program may use at most 64 MiB of HBM per device.

```python
import math
import jax
import jax.numpy as jnp
import numpy as np
from jax import lax

D = 2048
FF = 768
EXPERTS = 64
TOP = 2
ROWS_DEV = 128
BYTES_DEV = 256
CAP = 5
ROWS = 32768
BYTES = 65536
N_EXPERT = 64
N_DP = 4


def draw_positions(key, part):
    block_count = ROWS // ROWS_DEV
    key_list = jax.random.split(key, block_count)
    inner_count = ROWS_DEV - 2

    def one_block(block_key):
        order = jax.random.permutation(block_key, BYTES_DEV - 2)
        chosen = jnp.sort(order[:inner_count].astype(jnp.int32) + 1)
        head = jnp.zeros((1,), jnp.int32)
        tail = jnp.full((1,), BYTES_DEV - 1, jnp.int32)
        return jnp.concatenate([head, chosen, tail])
    local_pos = jax.vmap(one_block)(key_list)
    offsets = (jnp.arange(block_count, dtype=jnp.int32) * BYTES_DEV)[:, None]
    return (local_pos + offsets).reshape(ROWS)


def shard_levels(rng, dims, cuts, least, largest):
    def one(position, blocks):
        draws = jax.random.uniform(jax.random.fold_in(jax.random.fold_in(rng, 6), position), (blocks,), jnp.float32, least / len(cuts), largest / len(cuts))
        return jnp.repeat(jnp.exp(draws), dims[position] // blocks).reshape((-1,) + (1,) * (len(dims) - position - 1))

    level = one(*cuts[0])
    for cut in cuts[1:]:
        level = level * one(*cut)
    return level


def routed_block(own_key, own, number, rows, number_of, top, bound, lean):
    ranking = jax.random.permutation(own_key, number_of)
    heavy_load, common = load_shares(number_of, rows * top, bound, lean, True), load_shares(number_of, rows * top, bound, lean, False)
    places = jnp.arange(number_of)

    def named(tallies, turn):
        used = int((tallies > 0).sum())
        fixed = max(1, used // 4)
        passed = fixed + (places - fixed + turn * (used - fixed)) % max(1, number_of - fixed)
        return jnp.zeros((number_of,), jnp.int32).at[ranking[jnp.where(places < fixed, places, passed)]].set(jnp.asarray(tallies, jnp.int32))

    tallies = jnp.where(number % 4 == 0, named(heavy_load, number // 4), named(common, number - number // 4 - 1))
    mixed = jax.random.permutation(jax.random.fold_in(own, 3), number_of)
    donor, sink = mixed[0:number_of // 2 * 2:2], mixed[1:number_of // 2 * 2:2]
    margin = jnp.minimum(tallies[donor] - 1, bound - tallies[sink]) // 2
    margin = jnp.where((donor == ranking[0]) | (sink == ranking[0]) | (tallies[sink] == 0), 0, jnp.maximum(margin, 0))
    passed = jax.random.randint(jax.random.fold_in(own, 4), (number_of // 2,), 0, 1 << 20) % (margin + 1)
    tallies = tallies.at[donor].add(-passed).at[sink].add(passed)
    items = jnp.searchsorted(jnp.cumsum(tallies), jnp.arange(rows * top), side="right").astype(jnp.int32)
    listing = items.reshape(top, rows).T
    listing = listing[jax.random.permutation(jax.random.fold_in(own, 1), rows)]
    turn = jax.random.randint(jax.random.fold_in(own, 2), (rows, 1), 0, top)
    return jnp.take_along_axis(listing, (jnp.arange(top)[None, :] + turn) % top, axis=1)


def load_shares(amount, total, most, lean, full):
    weights = [(1 << 20) // math.isqrt(grade ** lean) + 1 for grade in range(1, amount + 1)]
    largest = most if full else min(most, max(-(-total // amount), total * weights[0] // sum(weights)))
    least = 1 if total - largest >= amount - 1 else 0
    holding, rest = [largest] + [least] * (amount - 1), total - largest - least * (amount - 1)
    while rest > 0:
        movable = [i for i in range(1, amount) if holding[i] < largest] or [i for i in range(1, amount) if holding[i] < most]
        mass, left = sum([weights[i] for i in movable]), rest
        for i in movable:
            more = min(most - holding[i], max(1, left * weights[i] // mass), rest)
            holding[i] = holding[i] + more
            rest = rest - more
    return np.array(holding)


def gaussian(key, shape, spread, reach, cuts=(), held_as=jnp.bfloat16):
    drawn = jax.random.normal(key, shape, jnp.float32) * spread
    if len(cuts) > 0:
        drawn = shard_levels(key, shape, cuts, -0.22, 0.18) * drawn
    return jnp.clip(drawn, min=-reach, max=reach).astype(held_as)


def setup_inputs(seed: int = 0) -> dict:
    keys = jax.random.split(jax.random.key(seed), 9)
    byte_states = gaussian(keys[0], (BYTES, D), 1.0, 6.0, ((0, 256),))
    positions = draw_positions(jax.random.fold_in(keys[8], 71), 0)
    picks_keys = jax.random.split(jax.random.fold_in(keys[2], 1), ROWS // ROWS_DEV)
    picks_turns = jax.random.permutation(jax.random.fold_in(keys[2], 3), ROWS // ROWS_DEV)
    picks = jax.vmap(lambda own, number: routed_block(jax.random.fold_in(keys[2], 2), own, number, ROWS_DEV, EXPERTS, TOP, CAP, 2))(picks_keys, picks_turns).reshape((ROWS, TOP))
    cotangent = gaussian(keys[3], (ROWS, D), 1.0, 6.0, ((0, 256),))
    router_weight = gaussian(keys[4], (D, EXPERTS), D ** -0.5, 0.125)
    gate_weight = gaussian(keys[5], (EXPERTS, D, FF), D ** -0.5, 0.125, ((0, 64), (1, 4), (2, 2)))
    up_weight = gaussian(keys[6], (EXPERTS, D, FF), D ** -0.5, 0.125, ((0, 64), (1, 4), (2, 2)))
    down_weight = gaussian(keys[7], (EXPERTS, D, FF), FF ** -0.5, 0.21875, ((0, 64), (1, 4), (2, 2)))
    return {"byte_states": byte_states, "positions": positions, "picks": picks, "cotangent": cotangent, "router_weight": router_weight, "gate_weight": gate_weight, "up_weight": up_weight, "down_weight": down_weight}


def reference(byte_states, positions, picks, cotangent, router_weight, gate_weight, up_weight, down_weight):
    boundary = jnp.take(byte_states, positions, axis=0)
    logits = jnp.dot(boundary, router_weight, preferred_element_type=jnp.float32)
    picked = jnp.take_along_axis(logits, picks, axis=1)
    leading = jax.nn.sigmoid(picked[:, 0] - picked[:, 1])
    mixing = jnp.stack([leading, 1.0 - leading], axis=1)
    mix_low = mixing.astype(jnp.bfloat16).reshape(-1)
    block_count = N_EXPERT * N_DP
    per_block = ROWS_DEV * TOP
    total = block_count * per_block
    flat_picks = picks.reshape(block_count, per_block)
    expert_ids = jnp.arange(EXPERTS, dtype=jnp.int32)
    one_hot = (flat_picks[:, :, None] == expert_ids[None, None, :]).astype(jnp.int32)
    slot_rank = jnp.sum(jnp.cumsum(one_hot, axis=1) * one_hot, axis=2) - 1
    block_ids = jnp.broadcast_to(jnp.arange(block_count, dtype=jnp.int32)[:, None], flat_picks.shape)
    pick_ids = jnp.arange(total, dtype=jnp.int32).reshape(block_count, per_block)
    slot_table = jnp.full((EXPERTS, block_count, CAP), total, jnp.int32)
    slot_table = slot_table.at[flat_picks, block_ids, slot_rank].set(pick_ids)

    def one_expert(expert_args):
        slot_ids, gate_mat, up_mat, down_mat = expert_args
        slot_ids = slot_ids.reshape(-1)
        is_live = slot_ids < total
        clamped = jnp.minimum(slot_ids, total - 1)
        source_row = clamped // TOP
        expert_rows = jnp.where(is_live[:, None], boundary[source_row], 0)
        expert_cot = jnp.where(is_live[:, None], cotangent[source_row], 0)
        expert_mix = jnp.where(is_live, mix_low[clamped], 0)
        gate_pre = jnp.dot(expert_rows, gate_mat, preferred_element_type=jnp.float32)
        up_pre = jnp.dot(expert_rows, up_mat, preferred_element_type=jnp.float32)
        sigma = jax.nn.sigmoid(gate_pre)
        activ = gate_pre * sigma
        slope = sigma * (1.0 + gate_pre * (1.0 - sigma))
        hidden = (activ * up_pre).astype(jnp.bfloat16)
        expert_out = lax.dot_general(hidden, down_mat, (((1,), (1,)), ((), ())), preferred_element_type=jnp.float32)
        mix_grad = jnp.sum(expert_cot.astype(jnp.float32) * expert_out, axis=1).astype(jnp.bfloat16)
        scaled = (expert_mix.astype(jnp.float32)[:, None] * expert_cot.astype(jnp.float32)).astype(jnp.bfloat16)
        hidden_grad = jnp.dot(scaled, down_mat, preferred_element_type=jnp.float32)
        gate_pre_grad = (hidden_grad * up_pre * slope).astype(jnp.bfloat16)
        up_pre_grad = (hidden_grad * activ).astype(jnp.bfloat16)
        pick_grad = lax.dot_general(gate_pre_grad, gate_mat, (((1,), (1,)), ((), ())), preferred_element_type=jnp.float32)
        pick_grad = pick_grad + lax.dot_general(up_pre_grad, up_mat, (((1,), (1,)), ((), ())), preferred_element_type=jnp.float32)
        pick_grad = pick_grad.astype(jnp.bfloat16)
        joined = jnp.concatenate([gate_pre_grad, up_pre_grad], axis=1)
        rows_four = expert_rows.reshape(N_EXPERT, N_DP, CAP, D).astype(jnp.float32)
        joined_four = joined.reshape(N_EXPERT, N_DP, CAP, 2 * FF).astype(jnp.float32)
        group_sums = jnp.einsum("sdcx,sdcf->dxf", rows_four, joined_four)
        rounded = lax.optimization_barrier(group_sums.astype(jnp.bfloat16))
        weight_sum = jnp.sum(rounded.astype(jnp.float32), axis=0).astype(jnp.bfloat16)
        return pick_grad, mix_grad, weight_sum[:, :FF], weight_sum[:, FF:]

    pick_all, mix_all, gate_grad, up_grad = lax.map(one_expert, (slot_table, gate_weight, up_weight, down_weight))
    flat_table = slot_table.reshape(EXPERTS, -1)
    pick_back = jnp.zeros((total, D), jnp.bfloat16).at[flat_table].set(pick_all, mode="drop")
    mix_back = jnp.zeros((total,), jnp.bfloat16).at[flat_table].set(mix_all, mode="drop")
    row_sum = jnp.sum(pick_back.reshape(ROWS, TOP, D).astype(jnp.float32), axis=1)
    mix_grad = mix_back.reshape(ROWS, TOP).astype(jnp.float32)
    blended = jnp.sum(mixing * mix_grad, axis=1, keepdims=True)
    logit_grad = mixing * (mix_grad - blended)
    pick_hot = (picks[:, :, None] == expert_ids[None, None, :]).astype(jnp.float32)
    coeffs = jnp.sum(logit_grad[:, :, None] * pick_hot, axis=1)
    router_term = jnp.dot(coeffs, router_weight.astype(jnp.float32).T, precision=lax.Precision.HIGHEST)
    row_grad = (row_sum + router_term).astype(jnp.bfloat16)
    return row_grad, gate_grad, up_grad
```

```python
import jax
import jax.numpy as jnp
from jax import lax
from jax.experimental import pallas as pl
from jax.experimental.pallas import tpu as pltpu
from jax.sharding import PartitionSpec as P


F32 = jnp.float32
BF16 = jnp.bfloat16
LANE = 128
VMEM_LIMIT = 24 * 1024 * 1024


def vm(x):
    return pltpu.with_memory_space_constraint(x, pltpu.VMEM)


def vspec():
    return pl.BlockSpec(memory_space=pltpu.VMEM)


def aspec():
    return pl.BlockSpec(memory_space=pl.ANY)


def sspec():
    return pl.BlockSpec(memory_space=pltpu.SMEM)


def params():
    return pltpu.CompilerParams(vmem_limit_bytes=VMEM_LIMIT)


def iota(shape, dim):
    return lax.broadcasted_iota(jnp.int32, shape, dim)


def dot(a, b):
    return jnp.dot(a, b, preferred_element_type=F32)


def dot_nt(a, b):
    return lax.dot_general(a, b, (((1,), (1,)), ((), ())), preferred_element_type=F32)


def dot_tn(a, b):
    return lax.dot_general(a, b, (((0,), (0,)), ((), ())), preferred_element_type=F32)


def local(
    byte_states, positions, picks, cotangent, router_weight, gate_weight, up_weight, down_weight
):
    byte_count, width = byte_states.shape
    rows = positions.shape[0]
    experts = router_weight.shape[1]
    cap = 5
    slots = cap * experts
    half = width // 2
    hc = half // LANE
    shard, fh = gate_weight.shape[1], gate_weight.shape[2]
    dps = width // shard
    disp = cap * 2 * hc
    back = cap * hc + 8

    pair = lax.axis_index("pair").astype(jnp.int32)
    dp = lax.axis_index("dp").astype(jnp.int32)
    idx = jnp.stack([pair, dp])

    def dispatch_kernel(
        idx_ref, bytes_ref, pos_ref, picks_ref, cot_ref, router_ref, out_ref, meta_ref, bnd, scr
    ):
        off = pl.multiple_of(idx_ref[0] * half, half)
        pos = jnp.bitwise_and(pos_ref[...], byte_count - 1)
        pos_hot = jnp.where(iota((byte_count, rows), 0) == pos, 1.0, 0.0).astype(BF16)
        bnd[...] = dot_tn(pos_hot, bytes_ref[...]).astype(BF16)
        p0 = picks_ref[0:1, :]
        p1 = picks_ref[1:2, :]
        ids = iota((experts, rows), 0)
        hot0 = jnp.where(ids == p0, 1.0, 0.0)
        hot1 = jnp.where(ids == p1, 1.0, 0.0)
        before = jnp.where(iota((rows, rows), 0) < iota((rows, rows), 1), 1.0, 0.0).astype(BF16)
        counts = dot((hot0 + hot1).astype(BF16), before)
        rank0 = jnp.sum(hot0 * counts, axis=0, keepdims=True)
        rank1 = jnp.sum(hot1 * counts, axis=0, keepdims=True)
        target0 = rank0 * experts + p0.astype(F32)
        target1 = rank1 * experts + p1.astype(F32)
        logits = dot_nt(router_ref[...], bnd[...])
        l0 = jnp.sum(hot0 * logits, axis=0, keepdims=True)
        l1 = jnp.sum(hot1 * logits, axis=0, keepdims=True)
        mix0 = jax.nn.sigmoid(l0 - l1)
        mix1 = 1.0 - mix0
        low0 = mix0.astype(BF16).astype(F32)
        low1 = mix1.astype(BF16).astype(F32)
        slot_ids = iota((slots, rows), 0).astype(F32)
        sel0 = slot_ids == target0
        sel1 = slot_ids == target1
        take = (jnp.where(sel0, 1.0, 0.0) + jnp.where(sel1, 1.0, 0.0)).astype(BF16)
        take_mix = (jnp.where(sel0, low0, 0.0) + jnp.where(sel1, low1, 0.0)).astype(BF16)
        send = (dot(take, bnd[:, pl.ds(off, half)]), dot(take_mix, cot_ref[:, pl.ds(off, half)]))
        for s in range(cap):
            for t in range(2):
                for c in range(hc):
                    scr[pl.ds((s * 2 + t) * hc + c, experts, stride=disp), :] = send[t][
                        s * experts : (s + 1) * experts, c * LANE : (c + 1) * LANE
                    ]
        out_ref[...] = scr[...].astype(BF16)
        meta_ref[...] = jnp.concatenate(
            [target0, target1, mix0, mix1, p0.astype(F32), p1.astype(F32), mix0, mix1], axis=0
        )

    payload, meta = pl.pallas_call(
        dispatch_kernel,
        out_shape=(
            jax.ShapeDtypeStruct((experts * disp, LANE), BF16),
            pltpu.VMEM((8, rows), F32),
        ),
        in_specs=[sspec()] + [vspec()] * 5,
        out_specs=(vspec(), vspec()),
        scratch_shapes=[pltpu.VMEM((rows, width), BF16), pltpu.VMEM((experts * disp, LANE), F32)],
        compiler_params=params(),
        name="dispatch",
    )(
        idx,
        byte_states,
        positions.reshape(1, rows),
        picks.T,
        cotangent,
        router_weight.T,
    )

    def exchange(x, count):
        return lax.all_to_all(
            x.reshape(experts, count, LANE), "expert", split_axis=0, concat_axis=0, tiled=True
        ).reshape(experts * count, LANE)

    recv = exchange(payload, disp)

    def aux_kernel(idx_ref, meta_ref, router_ref, hot_ref, delta_ref, mix_ref):
        off = pl.multiple_of(idx_ref[0] * half, half)
        slot_ids = iota((3 * LANE, rows), 0).astype(F32)
        for k in range(2):
            hot = jnp.where(slot_ids == meta_ref[k : k + 1, :], 1.0, 0.0)
            hot_ref[k * rows : (k + 1) * rows, :] = hot.T.astype(BF16)
        ids = iota((LANE, rows), 0).astype(F32)
        diff = jnp.where(ids == meta_ref[4:5, :], 1.0, 0.0) - jnp.where(
            ids == meta_ref[5:6, :], 1.0, 0.0
        )
        diff = diff.T.astype(BF16)[:, :experts]
        delta_ref[...] = dot(diff, router_ref[:, pl.ds(off, half)])
        cols = jnp.concatenate([meta_ref[...], jnp.zeros((LANE - 8, rows), F32)], axis=0)
        mix_ref[...] = cols.T

    hots, delta, mix_cols = pl.pallas_call(
        aux_kernel,
        out_shape=(
            jax.ShapeDtypeStruct((2 * rows, 3 * LANE), BF16),
            jax.ShapeDtypeStruct((rows, half), F32),
            jax.ShapeDtypeStruct((rows, LANE), F32),
        ),
        in_specs=[sspec()] + [vspec()] * 2,
        out_specs=(vspec(),) * 3,
        compiler_params=params(),
        name="aux",
    )(idx, vm(meta), router_weight.T)

    weights = jnp.stack([gate_weight[0], up_weight[0], down_weight[0]])
    pieces = [weights]
    for k in range(1, dps):
        pieces.append(lax.ppermute(weights, "dp", [(i, (i - k) % dps) for i in range(dps)]))

    def assemble_kernel(idx_ref, *refs):
        out_ref = refs[dps]
        y = idx_ref[1]
        for k in range(dps):
            row = pl.multiple_of(((y + k) % dps) * shard, shard)
            out_ref[:, pl.ds(row, shard), :] = refs[k][...]

    full = pl.pallas_call(
        assemble_kernel,
        out_shape=jax.ShapeDtypeStruct((3, width, fh), BF16),
        in_specs=[sspec()] + [vspec()] * dps,
        out_specs=vspec(),
        compiler_params=params(),
        name="assemble",
    )(idx, *[vm(x) for x in pieces])

    swap = [(0, 1), (1, 0)]
    recv_other = lax.ppermute(recv, "pair", swap)

    def unpack(ref, wide, x_dst, s_dst):
        wide[...] = ref[...].astype(F32)
        for s in range(cap):
            for t, dst in ((0, x_dst), (1, s_dst)):
                for c in range(hc):
                    val = wide[pl.ds((s * 2 + t) * hc + c, experts, stride=disp), :]
                    dst[s * experts : (s + 1) * experts, c * LANE : (c + 1) * LANE] = val.astype(
                        BF16
                    )

    def fetch(w_hbm, w_buf, sem, h, count):
        row = pl.multiple_of(h * half, half)
        return pltpu.make_async_copy(w_hbm.at[pl.ds(0, count), pl.ds(row, half), :], w_buf, sem)

    def own_kernel(idx_ref, recv_ref, w_hbm, x_ref, pre_ref, wide, s_buf, w_buf, sem):
        load = fetch(w_hbm, w_buf, sem, idx_ref[0], 3)
        load.start()
        unpack(recv_ref, wide, x_ref, s_buf)
        load.wait()
        pre_ref[0] = dot(x_ref[...], w_buf[0])
        pre_ref[1] = dot(x_ref[...], w_buf[1])
        pre_ref[2] = dot(s_buf[...], w_buf[2])

    x_own, pre = pl.pallas_call(
        own_kernel,
        out_shape=(
            pltpu.VMEM((slots, half), BF16),
            pltpu.VMEM((3, slots, fh), F32),
        ),
        in_specs=[sspec(), vspec(), aspec()],
        out_specs=(vspec(),) * 2,
        scratch_shapes=[
            pltpu.VMEM((experts * disp, LANE), F32),
            pltpu.VMEM((slots, half), BF16),
            pltpu.VMEM((3, half, fh), BF16),
            pltpu.SemaphoreType.DMA(()),
        ],
        compiler_params=params(),
        name="own",
    )(idx, vm(recv), full)

    def grads_kernel(
        idx_ref, recv_ref, w_hbm, pre_ref, x_ref, joined_ref, send_ref, mixed_ref, wide, s_buf, w_buf, sem
    ):
        load = fetch(w_hbm, w_buf, sem, 1 - idx_ref[0], 3)
        load.start()
        unpack(recv_ref, wide, x_ref, s_buf)
        load.wait()
        gate = pre_ref[0] + dot(x_ref[...], w_buf[0])
        up = pre_ref[1] + dot(x_ref[...], w_buf[1])
        grad = pre_ref[2] + dot(s_buf[...], w_buf[2])
        sigma = jax.nn.sigmoid(gate)
        activ = gate * sigma
        slope = sigma * (1.0 + gate * (1.0 - sigma))
        hidden = (activ * up).astype(BF16).astype(F32)
        mixed = jnp.sum(hidden * grad, axis=1, keepdims=True)
        gate_grad = (grad * up * slope).astype(BF16)
        up_grad = (grad * activ).astype(BF16)
        joined_ref[:, :fh] = gate_grad
        joined_ref[:, fh:] = up_grad
        send_ref[:, :half] = (
            dot_nt(gate_grad, w_buf[0]) + dot_nt(up_grad, w_buf[1])
        ).astype(BF16)
        wide_mixed = jnp.broadcast_to(mixed, (slots, LANE))
        high = wide_mixed.astype(BF16).astype(F32)
        mixed_ref[...] = wide_mixed
        send_ref[:, half:] = jnp.where(
            iota((slots, LANE), 1) < LANE // 2, high, wide_mixed - high
        ).astype(BF16)

    x_other, joined, send, mixed = pl.pallas_call(
        grads_kernel,
        out_shape=(
            pltpu.VMEM((slots, half), BF16),
            pltpu.VMEM((slots, 2 * fh), BF16),
            pltpu.VMEM((slots, half + LANE), BF16),
            pltpu.VMEM((slots, LANE), F32),
        ),
        in_specs=[sspec(), vspec(), aspec(), vspec()],
        out_specs=(vspec(),) * 4,
        scratch_shapes=[
            pltpu.VMEM((experts * disp, LANE), F32),
            pltpu.VMEM((slots, half), BF16),
            pltpu.VMEM((3, half, fh), BF16),
            pltpu.SemaphoreType.DMA(()),
        ],
        compiler_params=params(),
        name="grads",
    )(idx, vm(recv_other), full, vm(pre))

    sent = lax.ppermute(send, "pair", swap)

    def keep_kernel(idx_ref, joined_ref, w_hbm, keep_ref, w_buf, sem):
        load = fetch(w_hbm, w_buf, sem, idx_ref[0], 2)
        load.start()
        load.wait()
        keep_ref[...] = dot_nt(joined_ref[:, :fh], w_buf[0]) + dot_nt(joined_ref[:, fh:], w_buf[1])

    keep = pl.pallas_call(
        keep_kernel,
        out_shape=pltpu.VMEM((slots, half), F32),
        in_specs=[sspec(), vspec(), aspec()],
        out_specs=vspec(),
        scratch_shapes=[pltpu.VMEM((2, half, fh), BF16), pltpu.SemaphoreType.DMA(())],
        compiler_params=params(),
        name="keep",
    )(idx, vm(joined), full)

    def weight_kernel(idx_ref, own_ref, oth_ref, joined_ref, *refs):
        outs = refs[:dps]
        x_all = refs[dps]
        p = idx_ref[0]
        y = idx_ref[1]
        x_all[:, pl.ds(pl.multiple_of(p * half, half), half)] = own_ref[...]
        x_all[:, pl.ds(pl.multiple_of((1 - p) * half, half), half)] = oth_ref[...]
        for k in range(dps):
            col = pl.multiple_of(((y + k) % dps) * shard, shard)
            outs[k][...] = dot_tn(x_all[:, pl.ds(col, shard)], joined_ref[...]).astype(BF16)

    sums = pl.pallas_call(
        weight_kernel,
        out_shape=(pltpu.VMEM((shard, 2 * fh), BF16),) * dps,
        in_specs=[sspec()] + [vspec()] * 3,
        out_specs=(vspec(),) * dps,
        scratch_shapes=[pltpu.VMEM((slots, width), BF16)],
        compiler_params=params(),
        name="weight",
    )(idx, vm(x_own), vm(x_other), vm(joined))

    def pack_kernel(keep_ref, mixed_ref, sent_ref, out_ref, scr):
        for c in range(hc):
            lanes = slice(c * LANE, (c + 1) * LANE)
            total = keep_ref[:, lanes] + sent_ref[:, lanes].astype(F32)
            for s in range(cap):
                scr[pl.ds(s * hc + c, experts, stride=back), :] = total[
                    s * experts : (s + 1) * experts
                ]
        tail = sent_ref[:, half:].astype(F32)
        full = mixed_ref[...] + tail + pltpu.roll(tail, LANE // 2, 1)
        high = full.astype(BF16).astype(F32)
        both = jnp.where(iota((slots, LANE), 1) < LANE // 2, high, full - high)
        for s in range(8):
            part = both[s * experts : (s + 1) * experts] if s < cap else jnp.zeros((experts, LANE), F32)
            scr[pl.ds(cap * hc + s, experts, stride=back), :] = part
        out_ref[...] = scr[...].astype(BF16)

    packed = pl.pallas_call(
        pack_kernel,
        out_shape=jax.ShapeDtypeStruct((experts * back, LANE), BF16),
        in_specs=[vspec()] * 3,
        out_specs=vspec(),
        scratch_shapes=[pltpu.VMEM((experts * back, LANE), F32)],
        compiler_params=params(),
        name="pack",
    )(vm(keep), vm(mixed), vm(sent))

    returned = exchange(packed, back)

    moved = [sums[0]]
    for k in range(1, dps):
        moved.append(lax.ppermute(sums[k], "dp", [(i, (i + k) % dps) for i in range(dps)]))
    weight_sum = moved[0].astype(F32)
    for piece in moved[1:]:
        weight_sum = weight_sum + piece.astype(F32)
    weight_sum = weight_sum.astype(BF16)
    gate_out = weight_sum[:, :fh][None]
    up_out = weight_sum[:, fh:][None]

    def combine_kernel(back_ref, hot_ref, delta_ref, mix_ref, out_ref, wide, grads, small):
        wide[...] = back_ref[...].astype(F32)
        for s in range(cap):
            span = slice(s * experts, (s + 1) * experts)
            for c in range(hc):
                val = wide[pl.ds(s * hc + c, experts, stride=back), :]
                grads[span, c * LANE : (c + 1) * LANE] = val.astype(BF16)
            small[span, :] = wide[pl.ds(cap * hc + s, experts, stride=back), :].astype(BF16)
        grads[slots:, :] = jnp.zeros((3 * LANE - slots, half), BF16)
        small[slots:, :] = jnp.zeros((3 * LANE - slots, LANE), BF16)
        hot0 = hot_ref[:rows, :]
        hot1 = hot_ref[rows:, :]
        u0 = dot(hot0, small[...])
        u1 = dot(hot1, small[...])
        u0 = u0[:, 0:1] + u0[:, LANE // 2 : LANE // 2 + 1]
        u1 = u1[:, 0:1] + u1[:, LANE // 2 : LANE // 2 + 1]
        logit = mix_ref[:, 3:4] * u0 - mix_ref[:, 2:3] * u1
        out_ref[...] = (dot(hot0 + hot1, grads[...]) + logit * delta_ref[...]).astype(BF16)

    row_half = pl.pallas_call(
        combine_kernel,
        out_shape=jax.ShapeDtypeStruct((rows, half), BF16),
        in_specs=[vspec()] * 4,
        out_specs=vspec(),
        scratch_shapes=[
            pltpu.VMEM((experts * back, LANE), F32),
            pltpu.VMEM((3 * LANE, half), BF16),
            pltpu.VMEM((3 * LANE, LANE), BF16),
        ],
        compiler_params=params(),
        name="combine",
    )(vm(returned), hots, delta, mix_cols)

    row_half_other = lax.ppermute(row_half, "pair", swap)
    row_grad = jnp.where(
        pair == 0,
        jnp.concatenate([row_half, row_half_other], axis=1),
        jnp.concatenate([row_half_other, row_half], axis=1),
    )
    return (row_grad, gate_out, up_out)


def solution(mesh):
    in_specs = (
        P(("expert", "dp"), None),
        P(("expert", "dp")),
        P(("expert", "dp"), None),
        P(("expert", "dp"), None),
        P(),
        P("expert", "dp", "pair"),
        P("expert", "dp", "pair"),
        P("expert", "dp", "pair"),
    )
    out_specs = (P(("expert", "dp"), None), P("expert", "dp", "pair"), P("expert", "dp", "pair"))

    return jax.shard_map(local, mesh=mesh, in_specs=in_specs, out_specs=out_specs, check_vma=False)
```

```python
import jax
import jax.numpy as jnp
from jax import lax
from jax.experimental import pallas as pl
from jax.experimental.pallas import tpu as pltpu
from jax.sharding import PartitionSpec as P


F32 = jnp.float32
BF16 = jnp.bfloat16
LANE = 128
VMEM_LIMIT = 24 * 1024 * 1024


def vm(x):
    return pltpu.with_memory_space_constraint(x, pltpu.VMEM)


def hb(x):
    return pltpu.with_memory_space_constraint(x, pltpu.HBM)


def vspec():
    return pl.BlockSpec(memory_space=pltpu.VMEM)


def aspec():
    return pl.BlockSpec(memory_space=pl.ANY)


def pair_id():
    return lax.axis_index("pair").astype(jnp.int32)


def dp_id():
    return lax.axis_index("dp").astype(jnp.int32)


def params():
    return pltpu.CompilerParams(vmem_limit_bytes=VMEM_LIMIT)


def iota(shape, dim):
    return lax.broadcasted_iota(jnp.int32, shape, dim)


def dot(a, b):
    return jnp.dot(a, b, preferred_element_type=F32)


def dot_nt(a, b):
    return lax.dot_general(a, b, (((1,), (1,)), ((), ())), preferred_element_type=F32)


def dot_tn(a, b):
    return lax.dot_general(a, b, (((0,), (0,)), ((), ())), preferred_element_type=F32)


def local(
    byte_states, positions, picks, cotangent, router_weight, gate_weight, up_weight, down_weight
):
    byte_count, width = byte_states.shape
    rows = positions.shape[0]
    experts = router_weight.shape[1]
    cap = 5
    slots = cap * experts
    half = width // 2
    hc = half // LANE
    shard, fh = gate_weight.shape[1], gate_weight.shape[2]
    dps = width // shard
    disp = cap * 2 * hc
    back = cap * hc + 2
    part = shard // 2

    def dispatch_kernel(
        bytes_hbm, pos_hbm, picks_hbm, cot_hbm, router_hbm, out_ref, meta_ref,
        bytes_ref, pos_ref, picks_ref, cot_ref, router_ref, bnd, scr, sems,
    ):
        off = pl.multiple_of(pair_id() * half, half)
        loads = [
            pltpu.make_async_copy(pos_hbm, pos_ref, sems.at[0]),
            pltpu.make_async_copy(picks_hbm, picks_ref, sems.at[1]),
            pltpu.make_async_copy(bytes_hbm, bytes_ref, sems.at[2]),
            pltpu.make_async_copy(router_hbm, router_ref, sems.at[3]),
            pltpu.make_async_copy(cot_hbm.at[:, pl.ds(off, half)], cot_ref, sems.at[4]),
        ]
        for load in loads:
            load.start()
        loads[0].wait()
        loads[1].wait()
        pos = jnp.bitwise_and(pos_ref[...], byte_count - 1)
        pos_hot = jnp.where(iota((byte_count, rows), 0) == pos, 1.0, 0.0).astype(BF16)
        p0 = picks_ref[0:1, :]
        p1 = picks_ref[1:2, :]
        ids = iota((experts, rows), 0)
        hot0 = jnp.where(ids == p0, 1.0, 0.0)
        hot1 = jnp.where(ids == p1, 1.0, 0.0)
        before = jnp.where(iota((rows, rows), 0) < iota((rows, rows), 1), 1.0, 0.0).astype(BF16)
        counts = dot((hot0 + hot1).astype(BF16), before)
        rank0 = jnp.sum(hot0 * counts, axis=0, keepdims=True)
        rank1 = jnp.sum(hot1 * counts, axis=0, keepdims=True)
        target0 = rank0 * experts + p0.astype(F32)
        target1 = rank1 * experts + p1.astype(F32)
        loads[2].wait()
        bnd[...] = dot_tn(pos_hot, bytes_ref[...]).astype(BF16)
        loads[3].wait()
        logits = dot_nt(router_ref[...], bnd[...])
        l0 = jnp.sum(hot0 * logits, axis=0, keepdims=True)
        l1 = jnp.sum(hot1 * logits, axis=0, keepdims=True)
        mix0 = jax.nn.sigmoid(l0 - l1)
        mix1 = 1.0 - mix0
        low0 = mix0.astype(BF16).astype(F32)
        low1 = mix1.astype(BF16).astype(F32)
        slot_ids = iota((slots, rows), 0).astype(F32)
        sel0 = slot_ids == target0
        sel1 = slot_ids == target1
        take = (jnp.where(sel0, 1.0, 0.0) + jnp.where(sel1, 1.0, 0.0)).astype(BF16)
        take_mix = (jnp.where(sel0, low0, 0.0) + jnp.where(sel1, low1, 0.0)).astype(BF16)
        loads[4].wait()
        send = (dot(take, bnd[:, pl.ds(off, half)]), dot(take_mix, cot_ref[...]))
        for s in range(cap):
            for t in range(2):
                for c in range(hc):
                    scr[pl.ds((s * 2 + t) * hc + c, experts, stride=disp), :] = send[t][
                        s * experts : (s + 1) * experts, c * LANE : (c + 1) * LANE
                    ]
        out_ref[...] = scr[...].astype(BF16)
        meta_ref[...] = jnp.concatenate(
            [target0, target1, mix0, mix1, p0.astype(F32), p1.astype(F32), mix0, mix1], axis=0
        )

    payload, meta = pl.pallas_call(
        dispatch_kernel,
        out_shape=(
            jax.ShapeDtypeStruct((experts * disp, LANE), BF16),
            pltpu.VMEM((8, rows), F32),
        ),
        in_specs=[aspec()] * 5,
        out_specs=(vspec(), vspec()),
        scratch_shapes=[
            pltpu.VMEM((byte_count, width), BF16),
            pltpu.VMEM((1, rows), jnp.int32),
            pltpu.VMEM((2, rows), jnp.int32),
            pltpu.VMEM((rows, half), BF16),
            pltpu.VMEM((experts, width), BF16),
            pltpu.VMEM((rows, width), BF16),
            pltpu.VMEM((experts * disp, LANE), F32),
            pltpu.SemaphoreType.DMA((5,)),
        ],
        compiler_params=params(),
        name="dispatch",
    )(
        hb(byte_states),
        hb(positions.reshape(1, rows)),
        hb(picks.T),
        hb(cotangent),
        hb(router_weight.T),
    )

    def exchange(x, count, sub):
        shape = x.shape
        x = x.reshape((experts, count // sub) + shape[1:])
        return lax.all_to_all(x, "expert", split_axis=0, concat_axis=0, tiled=True).reshape(shape)

    recv = exchange(payload, disp, 1)

    def aux_kernel(
        meta_ref, router_ref, hot_hbm, delta_hbm, mix_hbm, hot_ref, delta_ref, mix_ref, sems
    ):
        off = pl.multiple_of(pair_id() * half, half)
        slot_ids = iota((3 * LANE, rows), 0).astype(F32)
        for k in range(2):
            hot = jnp.where(slot_ids == meta_ref[k : k + 1, :], 1.0, 0.0)
            hot_ref[k * rows : (k + 1) * rows, :] = hot.T.astype(BF16)
        ids = iota((LANE, rows), 0).astype(F32)
        diff = jnp.where(ids == meta_ref[4:5, :], 1.0, 0.0) - jnp.where(
            ids == meta_ref[5:6, :], 1.0, 0.0
        )
        diff = diff.T.astype(BF16)[:, :experts]
        delta_ref[...] = dot(diff, router_ref[:, pl.ds(off, half)])
        cols = jnp.concatenate([meta_ref[...], jnp.zeros((LANE - 8, rows), F32)], axis=0)
        mix_ref[...] = cols.T
        copies = [
            pltpu.make_async_copy(hot_ref, hot_hbm, sems.at[0]),
            pltpu.make_async_copy(delta_ref, delta_hbm, sems.at[1]),
            pltpu.make_async_copy(mix_ref, mix_hbm, sems.at[2]),
        ]
        for copy in copies:
            copy.start()
        for copy in copies:
            copy.wait()

    hots, delta, mix_cols = pl.pallas_call(
        aux_kernel,
        out_shape=(
            pltpu.HBM((2 * rows, 3 * LANE), BF16),
            pltpu.HBM((rows, half), F32),
            pltpu.HBM((rows, LANE), F32),
        ),
        in_specs=[vspec()] * 2,
        out_specs=(aspec(),) * 3,
        scratch_shapes=[
            pltpu.VMEM((2 * rows, 3 * LANE), BF16),
            pltpu.VMEM((rows, half), F32),
            pltpu.VMEM((rows, LANE), F32),
            pltpu.SemaphoreType.DMA((3,)),
        ],
        compiler_params=params(),
        name="aux",
    )(vm(meta), router_weight.T)

    def stack_kernel(gate_hbm, up_hbm, down_hbm, low_ref, high_ref, sems):
        copies = []
        for i, src in enumerate((gate_hbm, up_hbm, down_hbm)):
            for j, dst in enumerate((low_ref, high_ref)):
                copies.append(
                    pltpu.make_async_copy(
                        src.at[0, pl.ds(j * part, part), :], dst.at[i], sems.at[2 * i + j]
                    )
                )
        for copy in copies:
            copy.start()
        for copy in copies:
            copy.wait()

    low, high = pl.pallas_call(
        stack_kernel,
        out_shape=(pltpu.VMEM((3, part, fh), BF16),) * 2,
        in_specs=[aspec()] * 3,
        out_specs=(vspec(),) * 2,
        scratch_shapes=[pltpu.SemaphoreType.DMA((6,))],
        compiler_params=params(),
        name="stack",
    )(hb(gate_weight), hb(up_weight), hb(down_weight))

    ahead = [(i, (i + 1) % dps) for i in range(dps)]
    behind = [(i, (i - 1) % dps) for i in range(dps)]
    low_prev = lax.ppermute(low, "dp", ahead)
    high_next = lax.ppermute(high, "dp", behind)
    high_prev = lax.ppermute(high, "dp", ahead)
    low_next = lax.ppermute(low, "dp", behind)
    low_far = lax.ppermute(low_prev, "dp", ahead)
    high_far = lax.ppermute(high_next, "dp", behind)
    pieces = (low, high, low_next, high_next, low_far, high_far, low_prev, high_prev)

    def assemble_kernel(*refs):
        out_hbm, sems = refs[2 * dps :]
        y = dp_id()
        copies = []
        for k in range(dps):
            for j in range(2):
                row = pl.multiple_of(((y + k) % dps) * shard + j * part, part)
                copies.append(
                    pltpu.make_async_copy(
                        refs[2 * k + j], out_hbm.at[:, pl.ds(row, part), :], sems.at[2 * k + j]
                    )
                )
        for copy in copies:
            copy.start()
        for copy in copies:
            copy.wait()

    full = pl.pallas_call(
        assemble_kernel,
        out_shape=pltpu.HBM((3, width, fh), BF16),
        in_specs=[vspec()] * (2 * dps),
        out_specs=aspec(),
        scratch_shapes=[pltpu.SemaphoreType.DMA((2 * dps,))],
        compiler_params=params(),
        name="assemble",
    )(*[vm(x) for x in pieces])

    swap = [(0, 1), (1, 0)]
    recv_other = lax.ppermute(recv, "pair", swap)

    def unpack(ref, wide, x_dst, s_dst):
        wide[...] = ref[...].astype(F32)
        for s in range(cap):
            for t, dst in ((0, x_dst), (1, s_dst)):
                for c in range(hc):
                    val = wide[pl.ds((s * 2 + t) * hc + c, experts, stride=disp), :]
                    dst[s * experts : (s + 1) * experts, c * LANE : (c + 1) * LANE] = val.astype(
                        BF16
                    )

    def fetch(w_hbm, w_buf, sem, h, count):
        row = pl.multiple_of(h * half, half)
        return pltpu.make_async_copy(w_hbm.at[pl.ds(0, count), pl.ds(row, half), :], w_buf, sem)

    def own_kernel(recv_ref, w_hbm, x_ref, pre_ref, wide, s_buf, w_buf, sem):
        load = fetch(w_hbm, w_buf, sem, pair_id(), 3)
        load.start()
        unpack(recv_ref, wide, x_ref, s_buf)
        load.wait()
        pre_ref[0] = dot(x_ref[...], w_buf[0])
        pre_ref[1] = dot(x_ref[...], w_buf[1])
        pre_ref[2] = dot(s_buf[...], w_buf[2])

    x_own, pre = pl.pallas_call(
        own_kernel,
        out_shape=(
            pltpu.VMEM((slots, half), BF16),
            pltpu.VMEM((3, slots, fh), F32),
        ),
        in_specs=[vspec(), aspec()],
        out_specs=(vspec(),) * 2,
        scratch_shapes=[
            pltpu.VMEM((experts * disp, LANE), F32),
            pltpu.VMEM((slots, half), BF16),
            pltpu.VMEM((3, half, fh), BF16),
            pltpu.SemaphoreType.DMA(()),
        ],
        compiler_params=params(),
        name="own",
    )(vm(recv), hb(full))

    def grads_kernel(
        recv_ref, w_hbm, pre_ref, x_ref, joined_ref, send_ref, mixed_ref, wide, s_buf, w_buf, sem
    ):
        load = fetch(w_hbm, w_buf, sem, 1 - pair_id(), 3)
        load.start()
        unpack(recv_ref, wide, x_ref, s_buf)
        load.wait()
        gate = pre_ref[0] + dot(x_ref[...], w_buf[0])
        up = pre_ref[1] + dot(x_ref[...], w_buf[1])
        grad = pre_ref[2] + dot(s_buf[...], w_buf[2])
        sigma = jax.nn.sigmoid(gate)
        activ = gate * sigma
        slope = sigma * (1.0 + gate * (1.0 - sigma))
        hidden = (activ * up).astype(BF16).astype(F32)
        mixed = jnp.sum(hidden * grad, axis=1, keepdims=True)
        gate_grad = (grad * up * slope).astype(BF16)
        up_grad = (grad * activ).astype(BF16)
        joined_ref[:, :fh] = gate_grad
        joined_ref[:, fh:] = up_grad
        send_ref[:, :half] = (
            dot_nt(gate_grad, w_buf[0]) + dot_nt(up_grad, w_buf[1])
        ).astype(BF16)
        wide_mixed = jnp.broadcast_to(mixed, (slots, LANE))
        high = wide_mixed.astype(BF16).astype(F32)
        mixed_ref[...] = wide_mixed
        send_ref[:, half:] = jnp.where(
            iota((slots, LANE), 1) < LANE // 2, high, wide_mixed - high
        ).astype(BF16)

    x_other, joined, send, mixed = pl.pallas_call(
        grads_kernel,
        out_shape=(
            pltpu.VMEM((slots, half), BF16),
            pltpu.VMEM((slots, 2 * fh), BF16),
            pltpu.VMEM((slots, half + LANE), BF16),
            pltpu.VMEM((slots, LANE), F32),
        ),
        in_specs=[vspec(), aspec(), vspec()],
        out_specs=(vspec(),) * 4,
        scratch_shapes=[
            pltpu.VMEM((experts * disp, LANE), F32),
            pltpu.VMEM((slots, half), BF16),
            pltpu.VMEM((3, half, fh), BF16),
            pltpu.SemaphoreType.DMA(()),
        ],
        compiler_params=params(),
        name="grads",
    )(vm(recv_other), hb(full), vm(pre))

    sent = lax.ppermute(send, "pair", swap)

    def keep_kernel(joined_ref, w_hbm, keep_ref, w_buf, sem):
        load = fetch(w_hbm, w_buf, sem, pair_id(), 2)
        load.start()
        load.wait()
        keep_ref[...] = dot_nt(joined_ref[:, :fh], w_buf[0]) + dot_nt(joined_ref[:, fh:], w_buf[1])

    keep = pl.pallas_call(
        keep_kernel,
        out_shape=pltpu.VMEM((slots, half), F32),
        in_specs=[vspec(), aspec()],
        out_specs=vspec(),
        scratch_shapes=[pltpu.VMEM((2, half, fh), BF16), pltpu.SemaphoreType.DMA(())],
        compiler_params=params(),
        name="keep",
    )(vm(joined), hb(full))

    def weight_kernel(own_ref, oth_ref, joined_ref, *refs):
        outs = refs[:dps]
        x_all = refs[dps]
        p = pair_id()
        y = dp_id()
        x_all[:, pl.ds(pl.multiple_of(p * half, half), half)] = own_ref[...]
        x_all[:, pl.ds(pl.multiple_of((1 - p) * half, half), half)] = oth_ref[...]
        for k in range(dps):
            col = pl.multiple_of(((y + k) % dps) * shard, shard)
            outs[k][...] = dot_tn(x_all[:, pl.ds(col, shard)], joined_ref[...]).astype(BF16)

    sums = pl.pallas_call(
        weight_kernel,
        out_shape=(pltpu.VMEM((shard, 2 * fh), BF16),) * dps,
        in_specs=[vspec()] * 3,
        out_specs=(vspec(),) * dps,
        scratch_shapes=[pltpu.VMEM((slots, width), BF16)],
        compiler_params=params(),
        name="weight",
    )(vm(x_own), vm(x_other), vm(joined))

    def pack_kernel(keep_ref, mixed_ref, sent_ref, out_ref, scr):
        for c in range(hc):
            lanes = slice(c * LANE, (c + 1) * LANE)
            total = keep_ref[:, lanes] + sent_ref[:, lanes].astype(F32)
            for s in range(cap):
                scr[pl.ds(s * hc + c, experts, stride=back), :] = total[
                    s * experts : (s + 1) * experts
                ]
        tail = sent_ref[:, half:].astype(F32)
        full_mixed = mixed_ref[...] + tail + pltpu.roll(tail, LANE // 2, 1)
        high_mixed = full_mixed.astype(BF16).astype(F32)
        lane = iota((experts, LANE), 1)
        line = jnp.zeros((experts, LANE), F32)
        for s in range(cap):
            span = slice(s * experts, (s + 1) * experts)
            line = jnp.where(lane == s, high_mixed[span], line)
            line = jnp.where(lane == LANE // 2 + s, full_mixed[span] - high_mixed[span], line)
        scr[pl.ds(cap * hc, experts, stride=back), :] = line
        scr[pl.ds(cap * hc + 1, experts, stride=back), :] = jnp.zeros((experts, LANE), F32)
        out_ref[...] = scr[...].reshape(experts * back // 2, 2, LANE).astype(BF16)

    packed = pl.pallas_call(
        pack_kernel,
        out_shape=jax.ShapeDtypeStruct((experts * back // 2, 2, LANE), BF16),
        in_specs=[vspec()] * 3,
        out_specs=vspec(),
        scratch_shapes=[pltpu.VMEM((experts * back, LANE), F32)],
        compiler_params=params(),
        name="pack",
    )(vm(keep), vm(mixed), vm(sent))

    returned = exchange(packed, back, 2)

    moved = [sums[0]]
    for k in range(1, dps):
        moved.append(lax.ppermute(sums[k], "dp", [(i, (i + k) % dps) for i in range(dps)]))

    def total_kernel(*refs):
        gate_ref, up_ref = refs[dps:]
        total = refs[0][...].astype(F32)
        for ref in refs[1:dps]:
            total = total + ref[...].astype(F32)
        total = total.astype(BF16)
        gate_ref[0] = total[:, :fh]
        up_ref[0] = total[:, fh:]

    gate_out, up_out = pl.pallas_call(
        total_kernel,
        out_shape=(jax.ShapeDtypeStruct((1, shard, fh), BF16),) * 2,
        in_specs=[vspec()] * dps,
        out_specs=(vspec(),) * 2,
        compiler_params=params(),
        name="total",
    )(*[vm(x) for x in moved])

    def combine_kernel(
        back_ref, hot_hbm, delta_hbm, mix_hbm, out_ref,
        wide, grads, small, hot_ref, delta_ref, mix_ref, sems,
    ):
        loads = [
            pltpu.make_async_copy(hot_hbm, hot_ref, sems.at[0]),
            pltpu.make_async_copy(mix_hbm, mix_ref, sems.at[1]),
            pltpu.make_async_copy(delta_hbm, delta_ref, sems.at[2]),
        ]
        for load in loads:
            load.start()
        wide[...] = back_ref[...].astype(F32).reshape(experts * back, LANE)
        lane = jnp.bitwise_and(iota((experts, LANE), 1), LANE // 2 - 1)
        line = wide[pl.ds(cap * hc, experts, stride=back), :]
        for s in range(cap):
            span = slice(s * experts, (s + 1) * experts)
            for c in range(hc):
                val = wide[pl.ds(s * hc + c, experts, stride=back), :]
                grads[span, c * LANE : (c + 1) * LANE] = val.astype(BF16)
            small[span, :] = jnp.where(lane == s, line, 0.0).astype(BF16)
        grads[slots:, :] = jnp.zeros((3 * LANE - slots, half), BF16)
        small[slots:, :] = jnp.zeros((3 * LANE - slots, LANE), BF16)
        for load in loads:
            load.wait()
        hot0 = hot_ref[:rows, :]
        hot1 = hot_ref[rows:, :]
        u0 = jnp.sum(dot(hot0, small[...]), axis=1, keepdims=True)
        u1 = jnp.sum(dot(hot1, small[...]), axis=1, keepdims=True)
        logit = mix_ref[:, 3:4] * u0 - mix_ref[:, 2:3] * u1
        out_ref[...] = (dot(hot0 + hot1, grads[...]) + logit * delta_ref[...]).astype(BF16)

    row_half = pl.pallas_call(
        combine_kernel,
        out_shape=pltpu.VMEM((rows, half), BF16),
        in_specs=[vspec()] + [aspec()] * 3,
        out_specs=vspec(),
        scratch_shapes=[
            pltpu.VMEM((experts * back, LANE), F32),
            pltpu.VMEM((3 * LANE, half), BF16),
            pltpu.VMEM((3 * LANE, LANE), BF16),
            pltpu.VMEM((2 * rows, 3 * LANE), BF16),
            pltpu.VMEM((rows, half), F32),
            pltpu.VMEM((rows, LANE), F32),
            pltpu.SemaphoreType.DMA((3,)),
        ],
        compiler_params=params(),
        name="combine",
    )(vm(returned), hb(hots), hb(delta), hb(mix_cols))

    row_half_other = lax.ppermute(row_half, "pair", swap)

    def join_kernel(own_ref, oth_ref, out_hbm, sems):
        p = pair_id()
        copies = [
            pltpu.make_async_copy(
                src, out_hbm.at[:, pl.ds(pl.multiple_of(h * half, half), half)], sems.at[i]
            )
            for i, (src, h) in enumerate(((own_ref, p), (oth_ref, 1 - p)))
        ]
        for copy in copies:
            copy.start()
        for copy in copies:
            copy.wait()

    row_grad = pl.pallas_call(
        join_kernel,
        out_shape=jax.ShapeDtypeStruct((rows, width), BF16),
        in_specs=[vspec()] * 2,
        out_specs=aspec(),
        scratch_shapes=[pltpu.SemaphoreType.DMA((2,))],
        compiler_params=params(),
        name="join",
    )(vm(row_half), vm(row_half_other))
    return (row_grad, gate_out, up_out)


def solution(mesh):
    in_specs = (
        P(("expert", "dp"), None),
        P(("expert", "dp")),
        P(("expert", "dp"), None),
        P(("expert", "dp"), None),
        P(),
        P("expert", "dp", "pair"),
        P("expert", "dp", "pair"),
        P("expert", "dp", "pair"),
    )
    out_specs = (P(("expert", "dp"), None), P("expert", "dp", "pair"), P("expert", "dp", "pair"))

    return jax.shard_map(local, mesh=mesh, in_specs=in_specs, out_specs=out_specs, check_vma=False)
```

```python
import jax
import jax.numpy as jnp
from jax import lax
from jax.experimental import pallas as pl
from jax.experimental.pallas import tpu as pltpu
from jax.sharding import PartitionSpec as P


F32 = jnp.float32
BF16 = jnp.bfloat16
LANE = 128
VMEM_LIMIT = 24 * 1024 * 1024


def vm(x):
    return pltpu.with_memory_space_constraint(x, pltpu.VMEM)


def hb(x):
    return pltpu.with_memory_space_constraint(x, pltpu.HBM)


def vspec():
    return pl.BlockSpec(memory_space=pltpu.VMEM)


def aspec():
    return pl.BlockSpec(memory_space=pl.ANY)


def pair_id():
    return lax.axis_index("pair").astype(jnp.int32)


def dp_id():
    return lax.axis_index("dp").astype(jnp.int32)


def params():
    return pltpu.CompilerParams(vmem_limit_bytes=VMEM_LIMIT)


def iota(shape, dim):
    return lax.broadcasted_iota(jnp.int32, shape, dim)


def dot(a, b):
    return jnp.dot(a, b, preferred_element_type=F32)


def dot_nt(a, b):
    return lax.dot_general(a, b, (((1,), (1,)), ((), ())), preferred_element_type=F32)


def dot_tn(a, b):
    return lax.dot_general(a, b, (((0,), (0,)), ((), ())), preferred_element_type=F32)


def local(
    byte_states, positions, picks, cotangent, router_weight, gate_weight, up_weight, down_weight
):
    byte_count, width = byte_states.shape
    rows = positions.shape[0]
    experts = router_weight.shape[1]
    cap = 5
    slots = cap * experts
    half = width // 2
    hc = half // LANE
    shard, fh = gate_weight.shape[1], gate_weight.shape[2]
    dps = width // shard
    disp = cap * 2 * hc
    back = cap * hc + 2
    part = shard // 2

    def dispatch_kernel(
        bytes_hbm, pos_hbm, picks_hbm, cot_hbm, router_hbm, out_hbm, meta_ref,
        bytes_ref, pos_ref, picks_ref, cot_ref, router_ref, bnd, scr, buf, sems,
    ):
        off = pl.multiple_of(pair_id() * half, half)
        loads = [
            pltpu.make_async_copy(pos_hbm, pos_ref, sems.at[0]),
            pltpu.make_async_copy(picks_hbm, picks_ref, sems.at[1]),
            pltpu.make_async_copy(bytes_hbm, bytes_ref, sems.at[2]),
            pltpu.make_async_copy(router_hbm, router_ref, sems.at[3]),
            pltpu.make_async_copy(cot_hbm.at[:, pl.ds(off, half)], cot_ref, sems.at[4]),
        ]
        for load in loads:
            load.start()
        loads[0].wait()
        loads[1].wait()
        pos = jnp.bitwise_and(pos_ref[...], byte_count - 1)
        pos_hot = jnp.where(iota((byte_count, rows), 0) == pos, 1.0, 0.0).astype(BF16)
        p0 = picks_ref[0:1, :]
        p1 = picks_ref[1:2, :]
        ids = iota((experts, rows), 0)
        hot0 = jnp.where(ids == p0, 1.0, 0.0)
        hot1 = jnp.where(ids == p1, 1.0, 0.0)
        before = jnp.where(iota((rows, rows), 0) < iota((rows, rows), 1), 1.0, 0.0).astype(BF16)
        counts = dot((hot0 + hot1).astype(BF16), before)
        rank0 = jnp.sum(hot0 * counts, axis=0, keepdims=True)
        rank1 = jnp.sum(hot1 * counts, axis=0, keepdims=True)
        target0 = rank0 * experts + p0.astype(F32)
        target1 = rank1 * experts + p1.astype(F32)
        slot_ids = iota((slots, rows), 0).astype(F32)
        sel0 = slot_ids == target0
        sel1 = slot_ids == target1

        def emit(t, send):
            for s in range(cap):
                for c in range(hc):
                    scr[t, pl.ds(s * hc + c, experts, stride=cap * hc), :] = send[
                        s * experts : (s + 1) * experts, c * LANE : (c + 1) * LANE
                    ]
            buf[t] = scr[t].astype(BF16).reshape(experts, cap * hc, LANE)
            store = pltpu.make_async_copy(
                buf.at[t], out_hbm.at[:, pl.ds(t * cap * hc, cap * hc), :], sems.at[5 + t]
            )
            store.start()
            return store

        loads[2].wait()
        bnd[...] = dot_tn(pos_hot, bytes_ref[...]).astype(BF16)
        take = (jnp.where(sel0, 1.0, 0.0) + jnp.where(sel1, 1.0, 0.0)).astype(BF16)
        stores = [emit(0, dot(take, bnd[:, pl.ds(off, half)]))]
        loads[3].wait()
        logits = dot_nt(router_ref[...], bnd[...])
        l0 = jnp.sum(hot0 * logits, axis=0, keepdims=True)
        l1 = jnp.sum(hot1 * logits, axis=0, keepdims=True)
        mix0 = jax.nn.sigmoid(l0 - l1)
        mix1 = 1.0 - mix0
        low0 = mix0.astype(BF16).astype(F32)
        low1 = mix1.astype(BF16).astype(F32)
        take_mix = (jnp.where(sel0, low0, 0.0) + jnp.where(sel1, low1, 0.0)).astype(BF16)
        loads[4].wait()
        stores.append(emit(1, dot(take_mix, cot_ref[...])))
        meta_ref[...] = jnp.concatenate(
            [target0, target1, mix0, mix1, p0.astype(F32), p1.astype(F32), mix0, mix1], axis=0
        )
        for store in stores:
            store.wait()

    payload, meta = pl.pallas_call(
        dispatch_kernel,
        out_shape=(
            pltpu.HBM((experts, disp, LANE), BF16),
            pltpu.VMEM((8, rows), F32),
        ),
        in_specs=[aspec()] * 5,
        out_specs=(aspec(), vspec()),
        scratch_shapes=[
            pltpu.VMEM((byte_count, width), BF16),
            pltpu.VMEM((1, rows), jnp.int32),
            pltpu.VMEM((2, rows), jnp.int32),
            pltpu.VMEM((rows, half), BF16),
            pltpu.VMEM((experts, width), BF16),
            pltpu.VMEM((rows, width), BF16),
            pltpu.VMEM((2, experts * cap * hc, LANE), F32),
            pltpu.VMEM((2, experts, cap * hc, LANE), BF16),
            pltpu.SemaphoreType.DMA((7,)),
        ],
        compiler_params=params(),
        name="dispatch",
    )(
        hb(byte_states),
        hb(positions.reshape(1, rows)),
        hb(picks.T),
        hb(cotangent),
        hb(router_weight.T),
    )

    def exchange(x):
        return lax.all_to_all(x, "expert", split_axis=0, concat_axis=0, tiled=True)

    recv = exchange(payload).reshape(experts * disp, LANE)

    def aux_kernel(
        meta_ref, router_ref, hot_hbm, delta_hbm, mix_hbm, hot_ref, delta_ref, mix_ref, sems
    ):
        off = pl.multiple_of(pair_id() * half, half)
        slot_ids = iota((3 * LANE, rows), 0).astype(F32)
        for k in range(2):
            hot = jnp.where(slot_ids == meta_ref[k : k + 1, :], 1.0, 0.0)
            hot_ref[k * rows : (k + 1) * rows, :] = hot.T.astype(BF16)
        ids = iota((LANE, rows), 0).astype(F32)
        diff = jnp.where(ids == meta_ref[4:5, :], 1.0, 0.0) - jnp.where(
            ids == meta_ref[5:6, :], 1.0, 0.0
        )
        diff = diff.T.astype(BF16)[:, :experts]
        delta_ref[...] = dot(diff, router_ref[:, pl.ds(off, half)])
        cols = jnp.concatenate([meta_ref[...], jnp.zeros((LANE - 8, rows), F32)], axis=0)
        mix_ref[...] = cols.T
        copies = [
            pltpu.make_async_copy(hot_ref, hot_hbm, sems.at[0]),
            pltpu.make_async_copy(delta_ref, delta_hbm, sems.at[1]),
            pltpu.make_async_copy(mix_ref, mix_hbm, sems.at[2]),
        ]
        for copy in copies:
            copy.start()
        for copy in copies:
            copy.wait()

    hots, delta, mix_cols = pl.pallas_call(
        aux_kernel,
        out_shape=(
            pltpu.HBM((2 * rows, 3 * LANE), BF16),
            pltpu.HBM((rows, half), F32),
            pltpu.HBM((rows, LANE), F32),
        ),
        in_specs=[vspec()] * 2,
        out_specs=(aspec(),) * 3,
        scratch_shapes=[
            pltpu.VMEM((2 * rows, 3 * LANE), BF16),
            pltpu.VMEM((rows, half), F32),
            pltpu.VMEM((rows, LANE), F32),
            pltpu.SemaphoreType.DMA((3,)),
        ],
        compiler_params=params(),
        name="aux",
    )(vm(meta), router_weight.T)

    def stack_kernel(gate_hbm, up_hbm, down_hbm, low_ref, high_ref, sems):
        copies = []
        for i, src in enumerate((gate_hbm, up_hbm, down_hbm)):
            for j, dst in enumerate((low_ref, high_ref)):
                copies.append(
                    pltpu.make_async_copy(
                        src.at[0, pl.ds(j * part, part), :], dst.at[i], sems.at[2 * i + j]
                    )
                )
        for copy in copies:
            copy.start()
        for copy in copies:
            copy.wait()

    low, high = pl.pallas_call(
        stack_kernel,
        out_shape=(pltpu.VMEM((3, part, fh), BF16),) * 2,
        in_specs=[aspec()] * 3,
        out_specs=(vspec(),) * 2,
        scratch_shapes=[pltpu.SemaphoreType.DMA((6,))],
        compiler_params=params(),
        name="stack",
    )(hb(gate_weight), hb(up_weight), hb(down_weight))

    ahead = [(i, (i + 1) % dps) for i in range(dps)]
    behind = [(i, (i - 1) % dps) for i in range(dps)]
    low_prev = lax.ppermute(low, "dp", ahead)
    high_next = lax.ppermute(high, "dp", behind)
    high_prev = lax.ppermute(high, "dp", ahead)
    low_next = lax.ppermute(low, "dp", behind)
    low_far = lax.ppermute(low_prev, "dp", ahead)
    high_far = lax.ppermute(high_next, "dp", behind)
    pieces = (low, high, low_next, high_next, low_far, high_far, low_prev, high_prev)

    def assemble_kernel(*refs):
        out_hbm, sems = refs[2 * dps :]
        y = dp_id()
        copies = []
        for k in range(dps):
            for j in range(2):
                row = pl.multiple_of(((y + k) % dps) * shard + j * part, part)
                copies.append(
                    pltpu.make_async_copy(
                        refs[2 * k + j], out_hbm.at[:, pl.ds(row, part), :], sems.at[2 * k + j]
                    )
                )
        for copy in copies:
            copy.start()
        for copy in copies:
            copy.wait()

    full = pl.pallas_call(
        assemble_kernel,
        out_shape=pltpu.HBM((3, width, fh), BF16),
        in_specs=[vspec()] * (2 * dps),
        out_specs=aspec(),
        scratch_shapes=[pltpu.SemaphoreType.DMA((2 * dps,))],
        compiler_params=params(),
        name="assemble",
    )(*[vm(x) for x in pieces])

    swap = [(0, 1), (1, 0)]
    recv_other = lax.ppermute(recv, "pair", swap)

    def unpack(ref, wide, x_dst, s_dst):
        wide[...] = ref[...].astype(F32)
        for s in range(cap):
            for t, dst in ((0, x_dst), (1, s_dst)):
                for c in range(hc):
                    val = wide[pl.ds((t * cap + s) * hc + c, experts, stride=disp), :]
                    dst[s * experts : (s + 1) * experts, c * LANE : (c + 1) * LANE] = val.astype(
                        BF16
                    )

    def fetch(w_hbm, w_buf, sem, h, count):
        row = pl.multiple_of(h * half, half)
        return pltpu.make_async_copy(w_hbm.at[pl.ds(0, count), pl.ds(row, half), :], w_buf, sem)

    def own_kernel(recv_ref, w_hbm, x_ref, pre_ref, w_buf, wide, s_buf, sem):
        load = fetch(w_hbm, w_buf, sem, pair_id(), 3)
        load.start()
        unpack(recv_ref, wide, x_ref, s_buf)
        load.wait()
        pre_ref[0] = dot(x_ref[...], w_buf[0])
        pre_ref[1] = dot(x_ref[...], w_buf[1])
        pre_ref[2] = dot(s_buf[...], w_buf[2])

    x_own, pre, w_own = pl.pallas_call(
        own_kernel,
        out_shape=(
            pltpu.VMEM((slots, half), BF16),
            pltpu.VMEM((3, slots, fh), F32),
            pltpu.VMEM((3, half, fh), BF16),
        ),
        in_specs=[vspec(), aspec()],
        out_specs=(vspec(),) * 3,
        scratch_shapes=[
            pltpu.VMEM((experts * disp, LANE), F32),
            pltpu.VMEM((slots, half), BF16),
            pltpu.SemaphoreType.DMA(()),
        ],
        compiler_params=params(),
        name="own",
    )(vm(recv), hb(full))

    def grads_kernel(
        recv_ref, w_hbm, pre_ref, x_ref, joined_ref, send_ref, mixed_ref, wide, s_buf, w_buf, sem
    ):
        load = fetch(w_hbm, w_buf, sem, 1 - pair_id(), 3)
        load.start()
        unpack(recv_ref, wide, x_ref, s_buf)
        load.wait()
        gate = pre_ref[0] + dot(x_ref[...], w_buf[0])
        up = pre_ref[1] + dot(x_ref[...], w_buf[1])
        grad = pre_ref[2] + dot(s_buf[...], w_buf[2])
        sigma = jax.nn.sigmoid(gate)
        activ = gate * sigma
        slope = sigma * (1.0 + gate * (1.0 - sigma))
        hidden = (activ * up).astype(BF16).astype(F32)
        mixed = jnp.sum(hidden * grad, axis=1, keepdims=True)
        gate_grad = (grad * up * slope).astype(BF16)
        up_grad = (grad * activ).astype(BF16)
        joined_ref[:, :fh] = gate_grad
        joined_ref[:, fh:] = up_grad
        send_ref[:, :half] = (
            dot_nt(gate_grad, w_buf[0]) + dot_nt(up_grad, w_buf[1])
        ).astype(BF16)
        wide_mixed = jnp.broadcast_to(mixed, (slots, LANE))
        high = wide_mixed.astype(BF16).astype(F32)
        mixed_ref[...] = wide_mixed
        send_ref[:, half:] = jnp.where(
            iota((slots, LANE), 1) < LANE // 2, high, wide_mixed - high
        ).astype(BF16)

    x_other, joined, send, mixed = pl.pallas_call(
        grads_kernel,
        out_shape=(
            pltpu.VMEM((slots, half), BF16),
            pltpu.VMEM((slots, 2 * fh), BF16),
            pltpu.VMEM((slots, half + LANE), BF16),
            pltpu.VMEM((slots, LANE), F32),
        ),
        in_specs=[vspec(), aspec(), vspec()],
        out_specs=(vspec(),) * 4,
        scratch_shapes=[
            pltpu.VMEM((experts * disp, LANE), F32),
            pltpu.VMEM((slots, half), BF16),
            pltpu.VMEM((3, half, fh), BF16),
            pltpu.SemaphoreType.DMA(()),
        ],
        compiler_params=params(),
        name="grads",
    )(vm(recv_other), hb(full), vm(pre))

    sent = lax.ppermute(send, "pair", swap)

    def keep_kernel(joined_ref, w_ref, keep_ref):
        keep_ref[...] = dot_nt(joined_ref[:, :fh], w_ref[0]) + dot_nt(joined_ref[:, fh:], w_ref[1])

    keep = pl.pallas_call(
        keep_kernel,
        out_shape=pltpu.VMEM((slots, half), F32),
        in_specs=[vspec()] * 2,
        out_specs=vspec(),
        compiler_params=params(),
        name="keep",
    )(vm(joined), vm(w_own))

    def weight_kernel(own_ref, oth_ref, joined_ref, mine, next_low, next_high, far_low, far_high, prev_low, prev_high, x_all):
        p = pair_id()
        y = dp_id()
        x_all[:, pl.ds(pl.multiple_of(p * half, half), half)] = own_ref[...]
        x_all[:, pl.ds(pl.multiple_of((1 - p) * half, half), half)] = oth_ref[...]
        for k, dst in (
            (2, (far_low, far_high)),
            (1, (next_low, next_high)),
            (3, (prev_low, prev_high)),
            (0, (mine.at[:part], mine.at[part:])),
        ):
            col = pl.multiple_of(((y + k) % dps) * shard, shard)
            block = dot_tn(x_all[:, pl.ds(col, shard)], joined_ref[...]).astype(BF16)
            dst[0][...] = block[:part]
            dst[1][...] = block[part:]

    mine, next_low, next_high, far_low, far_high, prev_low, prev_high = pl.pallas_call(
        weight_kernel,
        out_shape=(pltpu.VMEM((shard, 2 * fh), BF16),)
        + (pltpu.VMEM((part, 2 * fh), BF16),) * 6,
        in_specs=[vspec()] * 3,
        out_specs=(vspec(),) * 7,
        scratch_shapes=[pltpu.VMEM((slots, width), BF16)],
        compiler_params=params(),
        name="weight",
    )(vm(x_own), vm(x_other), vm(joined))

    far_low = lax.ppermute(far_low, "dp", ahead)
    far_high = lax.ppermute(far_high, "dp", behind)
    got_high = lax.ppermute(next_high, "dp", ahead)
    got_low = lax.ppermute(prev_low, "dp", behind)

    def add_kernel(a_ref, b_ref, c_ref, d_ref, low_ref, high_ref):
        low_ref[...] = (a_ref[...].astype(F32) + b_ref[...].astype(F32)).astype(BF16)
        high_ref[...] = (c_ref[...].astype(F32) + d_ref[...].astype(F32)).astype(BF16)

    sum_low, sum_high = pl.pallas_call(
        add_kernel,
        out_shape=(pltpu.VMEM((part, 2 * fh), BF16),) * 2,
        in_specs=[vspec()] * 4,
        out_specs=(vspec(),) * 2,
        compiler_params=params(),
        name="add",
    )(vm(next_low), vm(far_low), vm(prev_high), vm(far_high))

    sum_low = lax.ppermute(sum_low, "dp", ahead)
    sum_high = lax.ppermute(sum_high, "dp", behind)

    def pack_kernel(keep_ref, mixed_ref, sent_ref, out_ref, scr):
        for c in range(hc):
            lanes = slice(c * LANE, (c + 1) * LANE)
            total = keep_ref[:, lanes] + sent_ref[:, lanes].astype(F32)
            for s in range(cap):
                scr[pl.ds(s * hc + c, experts, stride=back), :] = total[
                    s * experts : (s + 1) * experts
                ]
        tail = sent_ref[:, half:].astype(F32)
        full_mixed = mixed_ref[...] + tail + pltpu.roll(tail, LANE // 2, 1)
        high_mixed = full_mixed.astype(BF16).astype(F32)
        lane = iota((experts, LANE), 1)
        line = jnp.zeros((experts, LANE), F32)
        for s in range(cap):
            span = slice(s * experts, (s + 1) * experts)
            line = jnp.where(lane == s, high_mixed[span], line)
            line = jnp.where(lane == LANE // 2 + s, full_mixed[span] - high_mixed[span], line)
        scr[pl.ds(cap * hc, experts, stride=back), :] = line
        scr[pl.ds(cap * hc + 1, experts, stride=back), :] = jnp.zeros((experts, LANE), F32)
        out_ref[...] = scr[...].reshape(experts * back // 2, 2, LANE).astype(BF16)

    packed = pl.pallas_call(
        pack_kernel,
        out_shape=jax.ShapeDtypeStruct((experts * back // 2, 2, LANE), BF16),
        in_specs=[vspec()] * 3,
        out_specs=vspec(),
        scratch_shapes=[pltpu.VMEM((experts * back, LANE), F32)],
        compiler_params=params(),
        name="pack",
    )(vm(keep), vm(mixed), vm(sent))

    returned = exchange(packed.reshape(experts, back // 2, 2, LANE)).reshape(packed.shape)

    def total_kernel(mine_ref, a_ref, b_ref, c_ref, d_ref, gate_ref, up_ref):
        for span, one, two in ((slice(0, part), a_ref, b_ref), (slice(part, shard), c_ref, d_ref)):
            total = mine_ref[span, :].astype(F32) + one[...].astype(F32) + two[...].astype(F32)
            total = total.astype(BF16)
            gate_ref[0, span, :] = total[:, :fh]
            up_ref[0, span, :] = total[:, fh:]

    gate_out, up_out = pl.pallas_call(
        total_kernel,
        out_shape=(jax.ShapeDtypeStruct((1, shard, fh), BF16),) * 2,
        in_specs=[vspec()] * 5,
        out_specs=(vspec(),) * 2,
        compiler_params=params(),
        name="total",
    )(*[vm(x) for x in (mine, sum_low, got_low, got_high, sum_high)])

    def combine_kernel(
        back_ref, hot_hbm, delta_hbm, mix_hbm, out_ref,
        wide, grads, small, hot_ref, delta_ref, mix_ref, sems,
    ):
        loads = [
            pltpu.make_async_copy(hot_hbm, hot_ref, sems.at[0]),
            pltpu.make_async_copy(mix_hbm, mix_ref, sems.at[1]),
            pltpu.make_async_copy(delta_hbm, delta_ref, sems.at[2]),
        ]
        for load in loads:
            load.start()
        wide[...] = back_ref[...].astype(F32).reshape(experts * back, LANE)
        lane = jnp.bitwise_and(iota((experts, LANE), 1), LANE // 2 - 1)
        line = wide[pl.ds(cap * hc, experts, stride=back), :]
        for s in range(cap):
            span = slice(s * experts, (s + 1) * experts)
            for c in range(hc):
                val = wide[pl.ds(s * hc + c, experts, stride=back), :]
                grads[span, c * LANE : (c + 1) * LANE] = val.astype(BF16)
            small[span, :] = jnp.where(lane == s, line, 0.0).astype(BF16)
        grads[slots:, :] = jnp.zeros((3 * LANE - slots, half), BF16)
        small[slots:, :] = jnp.zeros((3 * LANE - slots, LANE), BF16)
        for load in loads:
            load.wait()
        hot0 = hot_ref[:rows, :]
        hot1 = hot_ref[rows:, :]
        u0 = jnp.sum(dot(hot0, small[...]), axis=1, keepdims=True)
        u1 = jnp.sum(dot(hot1, small[...]), axis=1, keepdims=True)
        logit = mix_ref[:, 3:4] * u0 - mix_ref[:, 2:3] * u1
        out_ref[...] = (dot(hot0 + hot1, grads[...]) + logit * delta_ref[...]).astype(BF16)

    row_half = pl.pallas_call(
        combine_kernel,
        out_shape=pltpu.VMEM((rows, half), BF16),
        in_specs=[vspec()] + [aspec()] * 3,
        out_specs=vspec(),
        scratch_shapes=[
            pltpu.VMEM((experts * back, LANE), F32),
            pltpu.VMEM((3 * LANE, half), BF16),
            pltpu.VMEM((3 * LANE, LANE), BF16),
            pltpu.VMEM((2 * rows, 3 * LANE), BF16),
            pltpu.VMEM((rows, half), F32),
            pltpu.VMEM((rows, LANE), F32),
            pltpu.SemaphoreType.DMA((3,)),
        ],
        compiler_params=params(),
        name="combine",
    )(vm(returned), hb(hots), hb(delta), hb(mix_cols))

    row_half_other = lax.ppermute(row_half, "pair", swap)

    def join_kernel(own_ref, oth_ref, out_hbm, sems):
        p = pair_id()
        copies = [
            pltpu.make_async_copy(
                src, out_hbm.at[:, pl.ds(pl.multiple_of(h * half, half), half)], sems.at[i]
            )
            for i, (src, h) in enumerate(((own_ref, p), (oth_ref, 1 - p)))
        ]
        for copy in copies:
            copy.start()
        for copy in copies:
            copy.wait()

    row_grad = pl.pallas_call(
        join_kernel,
        out_shape=jax.ShapeDtypeStruct((rows, width), BF16),
        in_specs=[vspec()] * 2,
        out_specs=aspec(),
        scratch_shapes=[pltpu.SemaphoreType.DMA((2,))],
        compiler_params=params(),
        name="join",
    )(vm(row_half), vm(row_half_other))
    return (row_grad, gate_out, up_out)


def solution(mesh):
    in_specs = (
        P(("expert", "dp"), None),
        P(("expert", "dp")),
        P(("expert", "dp"), None),
        P(("expert", "dp"), None),
        P(),
        P("expert", "dp", "pair"),
        P("expert", "dp", "pair"),
        P("expert", "dp", "pair"),
    )
    out_specs = (P(("expert", "dp"), None), P("expert", "dp", "pair"), P("expert", "dp", "pair"))

    return jax.shard_map(local, mesh=mesh, in_specs=in_specs, out_specs=out_specs, check_vma=False)
```

```python
import jax
import jax.numpy as jnp
from jax import lax
from jax.experimental import pallas as pl
from jax.experimental.pallas import tpu as pltpu
from jax.sharding import PartitionSpec as P


F32 = jnp.float32
BF16 = jnp.bfloat16
LANE = 128
VMEM_LIMIT = 24 * 1024 * 1024


def vm(x):
    return pltpu.with_memory_space_constraint(x, pltpu.VMEM)


def hb(x):
    return pltpu.with_memory_space_constraint(x, pltpu.HBM)


def vspec():
    return pl.BlockSpec(memory_space=pltpu.VMEM)


def aspec():
    return pl.BlockSpec(memory_space=pl.ANY)


def pair_id():
    return lax.axis_index("pair").astype(jnp.int32)


def dp_id():
    return lax.axis_index("dp").astype(jnp.int32)


def params():
    return pltpu.CompilerParams(vmem_limit_bytes=VMEM_LIMIT)


def iota(shape, dim):
    return lax.broadcasted_iota(jnp.int32, shape, dim)


def dot(a, b):
    return jnp.dot(a, b, preferred_element_type=F32)


def dot_nt(a, b):
    return lax.dot_general(a, b, (((1,), (1,)), ((), ())), preferred_element_type=F32)


def dot_tn(a, b):
    return lax.dot_general(a, b, (((0,), (0,)), ((), ())), preferred_element_type=F32)


def local(
    byte_states, positions, picks, cotangent, router_weight, gate_weight, up_weight, down_weight
):
    byte_count, width = byte_states.shape
    rows = positions.shape[0]
    experts = router_weight.shape[1]
    cap = 5
    slots = cap * experts
    half = width // 2
    hc = half // LANE
    shard, fh = gate_weight.shape[1], gate_weight.shape[2]
    dps = width // shard
    disp = cap * 2 * hc
    back = cap * hc + 2
    part = shard // 2

    def dispatch_kernel(
        bytes_hbm, pos_hbm, picks_hbm, cot_hbm, router_hbm, out_hbm, meta_ref,
        bytes_ref, pos_ref, picks_ref, cot_ref, router_ref, bnd, scr, buf, sems,
    ):
        off = pl.multiple_of(pair_id() * half, half)
        loads = [
            pltpu.make_async_copy(pos_hbm, pos_ref, sems.at[0]),
            pltpu.make_async_copy(picks_hbm, picks_ref, sems.at[1]),
            pltpu.make_async_copy(bytes_hbm, bytes_ref, sems.at[2]),
            pltpu.make_async_copy(router_hbm, router_ref, sems.at[3]),
            pltpu.make_async_copy(cot_hbm.at[:, pl.ds(off, half)], cot_ref, sems.at[4]),
        ]
        for load in loads:
            load.start()
        loads[0].wait()
        loads[1].wait()
        pos = jnp.bitwise_and(pos_ref[...], byte_count - 1)
        pos_hot = jnp.where(iota((byte_count, rows), 0) == pos, 1.0, 0.0).astype(BF16)
        p0 = picks_ref[0:1, :]
        p1 = picks_ref[1:2, :]
        ids = iota((experts, rows), 0)
        hot0 = jnp.where(ids == p0, 1.0, 0.0)
        hot1 = jnp.where(ids == p1, 1.0, 0.0)
        before = jnp.where(iota((rows, rows), 0) < iota((rows, rows), 1), 1.0, 0.0).astype(BF16)
        counts = dot((hot0 + hot1).astype(BF16), before)
        rank0 = jnp.sum(hot0 * counts, axis=0, keepdims=True)
        rank1 = jnp.sum(hot1 * counts, axis=0, keepdims=True)
        target0 = rank0 * experts + p0.astype(F32)
        target1 = rank1 * experts + p1.astype(F32)
        slot_ids = iota((slots, rows), 0).astype(F32)
        sel0 = slot_ids == target0
        sel1 = slot_ids == target1

        def emit(t, send):
            for s in range(cap):
                for c in range(hc):
                    scr[t, pl.ds(s * hc + c, experts, stride=cap * hc + 1), :] = send[
                        s * experts : (s + 1) * experts, c * LANE : (c + 1) * LANE
                    ]
            for e in range(experts):
                row = e * (cap * hc + 1)
                buf[t, e] = scr[t, row : row + cap * hc, :].astype(BF16)
            store = pltpu.make_async_copy(
                buf.at[t], out_hbm.at[:, pl.ds(t * cap * hc, cap * hc), :], sems.at[5 + t]
            )
            store.start()
            return store

        loads[2].wait()
        bnd[...] = dot_tn(pos_hot, bytes_ref[...]).astype(BF16)
        take = (jnp.where(sel0, 1.0, 0.0) + jnp.where(sel1, 1.0, 0.0)).astype(BF16)
        stores = [emit(0, dot(take, bnd[:, pl.ds(off, half)]))]
        loads[3].wait()
        logits = dot_nt(router_ref[...], bnd[...])
        l0 = jnp.sum(hot0 * logits, axis=0, keepdims=True)
        l1 = jnp.sum(hot1 * logits, axis=0, keepdims=True)
        mix0 = jax.nn.sigmoid(l0 - l1)
        mix1 = 1.0 - mix0
        low0 = mix0.astype(BF16).astype(F32)
        low1 = mix1.astype(BF16).astype(F32)
        take_mix = (jnp.where(sel0, low0, 0.0) + jnp.where(sel1, low1, 0.0)).astype(BF16)
        loads[4].wait()
        stores.append(emit(1, dot(take_mix, cot_ref[...])))
        meta_ref[...] = jnp.concatenate(
            [target0, target1, mix0, mix1, p0.astype(F32), p1.astype(F32), mix0, mix1], axis=0
        )
        for store in stores:
            store.wait()

    payload, meta = pl.pallas_call(
        dispatch_kernel,
        out_shape=(
            pltpu.HBM((experts, disp, LANE), BF16),
            pltpu.VMEM((8, rows), F32),
        ),
        in_specs=[aspec()] * 5,
        out_specs=(aspec(), vspec()),
        scratch_shapes=[
            pltpu.VMEM((byte_count, width), BF16),
            pltpu.VMEM((1, rows), jnp.int32),
            pltpu.VMEM((2, rows), jnp.int32),
            pltpu.VMEM((rows, half), BF16),
            pltpu.VMEM((experts, width), BF16),
            pltpu.VMEM((rows, width), BF16),
            pltpu.VMEM((2, experts * (cap * hc + 1), LANE), F32),
            pltpu.VMEM((2, experts, cap * hc, LANE), BF16),
            pltpu.SemaphoreType.DMA((7,)),
        ],
        compiler_params=params(),
        name="dispatch",
    )(
        hb(byte_states),
        hb(positions.reshape(1, rows)),
        hb(picks.T),
        hb(cotangent),
        hb(router_weight.T),
    )

    def exchange(x):
        return lax.all_to_all(x, "expert", split_axis=0, concat_axis=0, tiled=True)

    recv = exchange(payload).reshape(experts * disp, LANE)

    def aux_kernel(
        meta_ref, router_ref, hot_hbm, delta_hbm, mix_hbm, hot_ref, delta_ref, mix_ref, sems
    ):
        off = pl.multiple_of(pair_id() * half, half)
        slot_ids = iota((3 * LANE, rows), 0).astype(F32)
        for k in range(2):
            hot = jnp.where(slot_ids == meta_ref[k : k + 1, :], 1.0, 0.0)
            hot_ref[k * rows : (k + 1) * rows, :] = hot.T.astype(BF16)
        ids = iota((LANE, rows), 0).astype(F32)
        diff = jnp.where(ids == meta_ref[4:5, :], 1.0, 0.0) - jnp.where(
            ids == meta_ref[5:6, :], 1.0, 0.0
        )
        diff = diff.T.astype(BF16)[:, :experts]
        delta_ref[...] = dot(diff, router_ref[:, pl.ds(off, half)])
        cols = jnp.concatenate([meta_ref[...], jnp.zeros((LANE - 8, rows), F32)], axis=0)
        mix_ref[...] = cols.T
        copies = [
            pltpu.make_async_copy(hot_ref, hot_hbm, sems.at[0]),
            pltpu.make_async_copy(delta_ref, delta_hbm, sems.at[1]),
            pltpu.make_async_copy(mix_ref, mix_hbm, sems.at[2]),
        ]
        for copy in copies:
            copy.start()
        for copy in copies:
            copy.wait()

    hots, delta, mix_cols = pl.pallas_call(
        aux_kernel,
        out_shape=(
            pltpu.HBM((2 * rows, 3 * LANE), BF16),
            pltpu.HBM((rows, half), F32),
            pltpu.HBM((rows, LANE), F32),
        ),
        in_specs=[vspec()] * 2,
        out_specs=(aspec(),) * 3,
        scratch_shapes=[
            pltpu.VMEM((2 * rows, 3 * LANE), BF16),
            pltpu.VMEM((rows, half), F32),
            pltpu.VMEM((rows, LANE), F32),
            pltpu.SemaphoreType.DMA((3,)),
        ],
        compiler_params=params(),
        name="aux",
    )(vm(meta), router_weight.T)

    def stack_kernel(gate_hbm, up_hbm, down_hbm, low_ref, high_ref, sems):
        copies = []
        for i, src in enumerate((gate_hbm, up_hbm, down_hbm)):
            for j, dst in enumerate((low_ref, high_ref)):
                copies.append(
                    pltpu.make_async_copy(
                        src.at[0, pl.ds(j * part, part), :], dst.at[i], sems.at[2 * i + j]
                    )
                )
        for copy in copies:
            copy.start()
        for copy in copies:
            copy.wait()

    low, high = pl.pallas_call(
        stack_kernel,
        out_shape=(pltpu.VMEM((3, part, fh), BF16),) * 2,
        in_specs=[aspec()] * 3,
        out_specs=(vspec(),) * 2,
        scratch_shapes=[pltpu.SemaphoreType.DMA((6,))],
        compiler_params=params(),
        name="stack",
    )(hb(gate_weight), hb(up_weight), hb(down_weight))

    ahead = [(i, (i + 1) % dps) for i in range(dps)]
    behind = [(i, (i - 1) % dps) for i in range(dps)]
    low_prev = lax.ppermute(low, "dp", ahead)
    high_next = lax.ppermute(high, "dp", behind)
    high_prev = lax.ppermute(high, "dp", ahead)
    low_next = lax.ppermute(low, "dp", behind)
    low_far = lax.ppermute(low_prev, "dp", ahead)
    high_far = lax.ppermute(high_next, "dp", behind)
    pieces = (low, high, low_next, high_next, low_far, high_far, low_prev, high_prev)

    def assemble_kernel(*refs):
        out_hbm, sems = refs[2 * dps :]
        y = dp_id()
        copies = []
        for k in range(dps):
            for j in range(2):
                row = pl.multiple_of(((y + k) % dps) * shard + j * part, part)
                copies.append(
                    pltpu.make_async_copy(
                        refs[2 * k + j], out_hbm.at[:, pl.ds(row, part), :], sems.at[2 * k + j]
                    )
                )
        for copy in copies:
            copy.start()
        for copy in copies:
            copy.wait()

    full = pl.pallas_call(
        assemble_kernel,
        out_shape=pltpu.HBM((3, width, fh), BF16),
        in_specs=[vspec()] * (2 * dps),
        out_specs=aspec(),
        scratch_shapes=[pltpu.SemaphoreType.DMA((2 * dps,))],
        compiler_params=params(),
        name="assemble",
    )(*[vm(x) for x in pieces])

    swap = [(0, 1), (1, 0)]
    recv_other = lax.ppermute(recv, "pair", swap)

    def unpack(ref, wide, x_dst, s_dst):
        for e in range(experts):
            wide[e * (disp + 1) : e * (disp + 1) + disp, :] = ref[
                e * disp : (e + 1) * disp, :
            ].astype(F32)
        for s in range(cap):
            for t, dst in ((0, x_dst), (1, s_dst)):
                for c in range(hc):
                    val = wide[pl.ds((t * cap + s) * hc + c, experts, stride=disp + 1), :]
                    dst[s * experts : (s + 1) * experts, c * LANE : (c + 1) * LANE] = val.astype(
                        BF16
                    )

    def fetch(w_hbm, w_buf, sem, h, count):
        row = pl.multiple_of(h * half, half)
        return pltpu.make_async_copy(w_hbm.at[pl.ds(0, count), pl.ds(row, half), :], w_buf, sem)

    def own_kernel(recv_ref, w_hbm, x_ref, pre_ref, w_buf, wide, s_buf, sem):
        load = fetch(w_hbm, w_buf, sem, pair_id(), 3)
        load.start()
        unpack(recv_ref, wide, x_ref, s_buf)
        load.wait()
        pre_ref[0] = dot(x_ref[...], w_buf[0])
        pre_ref[1] = dot(x_ref[...], w_buf[1])
        pre_ref[2] = dot(s_buf[...], w_buf[2])

    x_own, pre, w_own = pl.pallas_call(
        own_kernel,
        out_shape=(
            pltpu.VMEM((slots, half), BF16),
            pltpu.VMEM((3, slots, fh), F32),
            pltpu.VMEM((3, half, fh), BF16),
        ),
        in_specs=[vspec(), aspec()],
        out_specs=(vspec(),) * 3,
        scratch_shapes=[
            pltpu.VMEM((experts * (disp + 1), LANE), F32),
            pltpu.VMEM((slots, half), BF16),
            pltpu.SemaphoreType.DMA(()),
        ],
        compiler_params=params(),
        name="own",
    )(vm(recv), hb(full))

    def grads_kernel(
        recv_ref, w_hbm, pre_ref, x_ref, joined_ref, send_ref, mixed_ref, wide, s_buf, w_buf, sem
    ):
        load = fetch(w_hbm, w_buf, sem, 1 - pair_id(), 3)
        load.start()
        unpack(recv_ref, wide, x_ref, s_buf)
        load.wait()
        gate = pre_ref[0] + dot(x_ref[...], w_buf[0])
        up = pre_ref[1] + dot(x_ref[...], w_buf[1])
        grad = pre_ref[2] + dot(s_buf[...], w_buf[2])
        sigma = jax.nn.sigmoid(gate)
        activ = gate * sigma
        slope = sigma * (1.0 + gate * (1.0 - sigma))
        hidden = (activ * up).astype(BF16).astype(F32)
        mixed = jnp.sum(hidden * grad, axis=1, keepdims=True)
        gate_grad = (grad * up * slope).astype(BF16)
        up_grad = (grad * activ).astype(BF16)
        joined_ref[:, :fh] = gate_grad
        joined_ref[:, fh:] = up_grad
        send_ref[:, :half] = (
            dot_nt(gate_grad, w_buf[0]) + dot_nt(up_grad, w_buf[1])
        ).astype(BF16)
        wide_mixed = jnp.broadcast_to(mixed, (slots, LANE))
        high = wide_mixed.astype(BF16).astype(F32)
        mixed_ref[...] = wide_mixed
        send_ref[:, half:] = jnp.where(
            iota((slots, LANE), 1) < LANE // 2, high, wide_mixed - high
        ).astype(BF16)

    x_other, joined, send, mixed = pl.pallas_call(
        grads_kernel,
        out_shape=(
            pltpu.VMEM((slots, half), BF16),
            pltpu.VMEM((slots, 2 * fh), BF16),
            pltpu.VMEM((slots, half + LANE), BF16),
            pltpu.VMEM((slots, LANE), F32),
        ),
        in_specs=[vspec(), aspec(), vspec()],
        out_specs=(vspec(),) * 4,
        scratch_shapes=[
            pltpu.VMEM((experts * (disp + 1), LANE), F32),
            pltpu.VMEM((slots, half), BF16),
            pltpu.VMEM((3, half, fh), BF16),
            pltpu.SemaphoreType.DMA(()),
        ],
        compiler_params=params(),
        name="grads",
    )(vm(recv_other), hb(full), vm(pre))

    sent = lax.ppermute(send, "pair", swap)

    def keep_kernel(joined_ref, w_ref, keep_ref):
        keep_ref[...] = dot_nt(joined_ref[:, :fh], w_ref[0]) + dot_nt(joined_ref[:, fh:], w_ref[1])

    keep = pl.pallas_call(
        keep_kernel,
        out_shape=pltpu.VMEM((slots, half), F32),
        in_specs=[vspec()] * 2,
        out_specs=vspec(),
        compiler_params=params(),
        name="keep",
    )(vm(joined), vm(w_own))

    def weight_kernel(own_ref, oth_ref, joined_ref, mine, next_low, next_high, far_low, far_high, prev_low, prev_high, x_all):
        p = pair_id()
        y = dp_id()
        x_all[:, pl.ds(pl.multiple_of(p * half, half), half)] = own_ref[...]
        x_all[:, pl.ds(pl.multiple_of((1 - p) * half, half), half)] = oth_ref[...]
        for k, dst in (
            (2, (far_low, far_high)),
            (1, (next_low, next_high)),
            (3, (prev_low, prev_high)),
            (0, (mine.at[:part], mine.at[part:])),
        ):
            col = pl.multiple_of(((y + k) % dps) * shard, shard)
            block = dot_tn(x_all[:, pl.ds(col, shard)], joined_ref[...]).astype(BF16)
            dst[0][...] = block[:part]
            dst[1][...] = block[part:]

    mine, next_low, next_high, far_low, far_high, prev_low, prev_high = pl.pallas_call(
        weight_kernel,
        out_shape=(pltpu.VMEM((shard, 2 * fh), BF16),)
        + (pltpu.VMEM((part, 2 * fh), BF16),) * 6,
        in_specs=[vspec()] * 3,
        out_specs=(vspec(),) * 7,
        scratch_shapes=[pltpu.VMEM((slots, width), BF16)],
        compiler_params=params(),
        name="weight",
    )(vm(x_own), vm(x_other), vm(joined))

    far_low = lax.ppermute(far_low, "dp", ahead)
    far_high = lax.ppermute(far_high, "dp", behind)
    got_high = lax.ppermute(next_high, "dp", ahead)
    got_low = lax.ppermute(prev_low, "dp", behind)

    def add_kernel(a_ref, b_ref, c_ref, d_ref, low_ref, high_ref):
        low_ref[...] = (a_ref[...].astype(F32) + b_ref[...].astype(F32)).astype(BF16)
        high_ref[...] = (c_ref[...].astype(F32) + d_ref[...].astype(F32)).astype(BF16)

    sum_low, sum_high = pl.pallas_call(
        add_kernel,
        out_shape=(pltpu.VMEM((part, 2 * fh), BF16),) * 2,
        in_specs=[vspec()] * 4,
        out_specs=(vspec(),) * 2,
        compiler_params=params(),
        name="add",
    )(vm(next_low), vm(far_low), vm(prev_high), vm(far_high))

    sum_low = lax.ppermute(sum_low, "dp", ahead)
    sum_high = lax.ppermute(sum_high, "dp", behind)

    def pack_kernel(keep_ref, mixed_ref, sent_ref, out_ref):
        for s in range(cap):
            span = slice(s * experts, (s + 1) * experts)
            total = keep_ref[span, :] + sent_ref[span, :half].astype(F32)
            total = total.reshape(experts, hc, LANE).astype(BF16)
            out_ref[:, s * hc // 2 : (s + 1) * hc // 2] = total.reshape(experts, hc // 2, 2, LANE)
        tail = sent_ref[:, half:].astype(F32)
        full_mixed = mixed_ref[...] + tail + pltpu.roll(tail, LANE // 2, 1)
        high_mixed = full_mixed.astype(BF16).astype(F32)
        lane = iota((experts, LANE), 1)
        line = jnp.zeros((experts, LANE), F32)
        for s in range(cap):
            span = slice(s * experts, (s + 1) * experts)
            line = jnp.where(lane == s, high_mixed[span], line)
            line = jnp.where(lane == LANE // 2 + s, full_mixed[span] - high_mixed[span], line)
        line = jnp.stack([line, jnp.zeros((experts, LANE), F32)], axis=1)
        out_ref[:, back // 2 - 1 :] = line.reshape(experts, 1, 2, LANE).astype(BF16)

    packed = pl.pallas_call(
        pack_kernel,
        out_shape=jax.ShapeDtypeStruct((experts, back // 2, 2, LANE), BF16),
        in_specs=[vspec()] * 3,
        out_specs=vspec(),
        compiler_params=params(),
        name="pack",
    )(vm(keep), vm(mixed), vm(sent))

    returned = exchange(packed)

    def total_kernel(mine_ref, a_ref, b_ref, c_ref, d_ref, gate_ref, up_ref):
        for span, one, two in ((slice(0, part), a_ref, b_ref), (slice(part, shard), c_ref, d_ref)):
            total = mine_ref[span, :].astype(F32) + one[...].astype(F32) + two[...].astype(F32)
            total = total.astype(BF16)
            gate_ref[0, span, :] = total[:, :fh]
            up_ref[0, span, :] = total[:, fh:]

    gate_out, up_out = pl.pallas_call(
        total_kernel,
        out_shape=(jax.ShapeDtypeStruct((1, shard, fh), BF16),) * 2,
        in_specs=[vspec()] * 5,
        out_specs=(vspec(),) * 2,
        compiler_params=params(),
        name="total",
    )(*[vm(x) for x in (mine, sum_low, got_low, got_high, sum_high)])

    def combine_kernel(
        back_ref, hot_hbm, delta_hbm, mix_hbm, out_ref,
        grads, small, hot_ref, delta_ref, mix_ref, sems,
    ):
        loads = [
            pltpu.make_async_copy(hot_hbm, hot_ref, sems.at[0]),
            pltpu.make_async_copy(mix_hbm, mix_ref, sems.at[1]),
            pltpu.make_async_copy(delta_hbm, delta_ref, sems.at[2]),
        ]
        for load in loads:
            load.start()
        lane = jnp.bitwise_and(iota((experts, LANE), 1), LANE // 2 - 1)
        line = back_ref[:, back // 2 - 1 :].astype(F32).reshape(experts, 2 * LANE)[:, :LANE]
        for s in range(cap):
            span = slice(s * experts, (s + 1) * experts)
            block = back_ref[:, s * hc // 2 : (s + 1) * hc // 2].astype(F32)
            grads[span, :] = block.reshape(experts, half).astype(BF16)
            small[span, :] = jnp.where(lane == s, line, 0.0).astype(BF16)
        grads[slots:, :] = jnp.zeros((3 * LANE - slots, half), BF16)
        small[slots:, :] = jnp.zeros((3 * LANE - slots, LANE), BF16)
        for load in loads:
            load.wait()
        hot0 = hot_ref[:rows, :]
        hot1 = hot_ref[rows:, :]
        u0 = jnp.sum(dot(hot0, small[...]), axis=1, keepdims=True)
        u1 = jnp.sum(dot(hot1, small[...]), axis=1, keepdims=True)
        logit = mix_ref[:, 3:4] * u0 - mix_ref[:, 2:3] * u1
        out_ref[...] = (dot(hot0 + hot1, grads[...]) + logit * delta_ref[...]).astype(BF16)

    row_half = pl.pallas_call(
        combine_kernel,
        out_shape=pltpu.VMEM((rows, half), BF16),
        in_specs=[vspec()] + [aspec()] * 3,
        out_specs=vspec(),
        scratch_shapes=[
            pltpu.VMEM((3 * LANE, half), BF16),
            pltpu.VMEM((3 * LANE, LANE), BF16),
            pltpu.VMEM((2 * rows, 3 * LANE), BF16),
            pltpu.VMEM((rows, half), F32),
            pltpu.VMEM((rows, LANE), F32),
            pltpu.SemaphoreType.DMA((3,)),
        ],
        compiler_params=params(),
        name="combine",
    )(vm(returned), hb(hots), hb(delta), hb(mix_cols))

    row_half_other = lax.ppermute(row_half, "pair", swap)

    def join_kernel(own_ref, oth_ref, out_hbm, sems):
        p = pair_id()
        copies = [
            pltpu.make_async_copy(
                src, out_hbm.at[:, pl.ds(pl.multiple_of(h * half, half), half)], sems.at[i]
            )
            for i, (src, h) in enumerate(((own_ref, p), (oth_ref, 1 - p)))
        ]
        for copy in copies:
            copy.start()
        for copy in copies:
            copy.wait()

    row_grad = pl.pallas_call(
        join_kernel,
        out_shape=jax.ShapeDtypeStruct((rows, width), BF16),
        in_specs=[vspec()] * 2,
        out_specs=aspec(),
        scratch_shapes=[pltpu.SemaphoreType.DMA((2,))],
        compiler_params=params(),
        name="join",
    )(vm(row_half), vm(row_half_other))
    return (row_grad, gate_out, up_out)


def solution(mesh):
    in_specs = (
        P(("expert", "dp"), None),
        P(("expert", "dp")),
        P(("expert", "dp"), None),
        P(("expert", "dp"), None),
        P(),
        P("expert", "dp", "pair"),
        P("expert", "dp", "pair"),
        P("expert", "dp", "pair"),
    )
    out_specs = (P(("expert", "dp"), None), P("expert", "dp", "pair"), P("expert", "dp", "pair"))

    return jax.shard_map(local, mesh=mesh, in_specs=in_specs, out_specs=out_specs, check_vma=False)
```

```python
import jax
import jax.numpy as jnp
from jax import lax
from jax.experimental import pallas as pl
from jax.experimental.pallas import tpu as pltpu
from jax.sharding import PartitionSpec as P


F32 = jnp.float32
BF16 = jnp.bfloat16
LANE = 128
VMEM_LIMIT = 32 * 1024 * 1024


def vm(x):
    return pltpu.with_memory_space_constraint(x, pltpu.VMEM)


def hb(x):
    return pltpu.with_memory_space_constraint(x, pltpu.HBM)


def vspec():
    return pl.BlockSpec(memory_space=pltpu.VMEM)


def aspec():
    return pl.BlockSpec(memory_space=pl.ANY)


def pair_id():
    return lax.axis_index("pair").astype(jnp.int32)


def dp_id():
    return lax.axis_index("dp").astype(jnp.int32)


def params():
    return pltpu.CompilerParams(vmem_limit_bytes=VMEM_LIMIT)


def iota(shape, dim):
    return lax.broadcasted_iota(jnp.int32, shape, dim)


def dot(a, b):
    return jnp.dot(a, b, preferred_element_type=F32)


def dot_nt(a, b):
    return lax.dot_general(a, b, (((1,), (1,)), ((), ())), preferred_element_type=F32)


def dot_tn(a, b):
    return lax.dot_general(a, b, (((0,), (0,)), ((), ())), preferred_element_type=F32)


def local(
    byte_states, positions, picks, cotangent, router_weight, gate_weight, up_weight, down_weight
):
    byte_count, width = byte_states.shape
    rows = positions.shape[0]
    experts = router_weight.shape[1]
    cap = 5
    slots = cap * experts
    half = width // 2
    hc = half // LANE
    shard, fh = gate_weight.shape[1], gate_weight.shape[2]
    dps = width // shard
    disp = cap * 2 * hc
    back = cap * hc + 2
    part = shard // 2

    def dispatch_kernel(
        bytes_hbm, pos_hbm, picks_hbm, cot_hbm, router_hbm, out_hbm, meta_ref,
        bytes_ref, pos_ref, picks_ref, cot_ref, router_ref, bnd, scr, buf, sems,
    ):
        off = pl.multiple_of(pair_id() * half, half)
        loads = [
            pltpu.make_async_copy(pos_hbm, pos_ref, sems.at[0]),
            pltpu.make_async_copy(picks_hbm, picks_ref, sems.at[1]),
            pltpu.make_async_copy(bytes_hbm, bytes_ref, sems.at[2]),
            pltpu.make_async_copy(router_hbm, router_ref, sems.at[3]),
            pltpu.make_async_copy(cot_hbm.at[:, pl.ds(off, half)], cot_ref, sems.at[4]),
        ]
        for load in loads:
            load.start()
        loads[0].wait()
        loads[1].wait()
        pos = jnp.bitwise_and(pos_ref[...], byte_count - 1)
        pos_hot = jnp.where(iota((byte_count, rows), 0) == pos, 1.0, 0.0).astype(BF16)
        p0 = picks_ref[0:1, :]
        p1 = picks_ref[1:2, :]
        ids = iota((experts, rows), 0)
        hot0 = jnp.where(ids == p0, 1.0, 0.0)
        hot1 = jnp.where(ids == p1, 1.0, 0.0)
        before = jnp.where(iota((rows, rows), 0) < iota((rows, rows), 1), 1.0, 0.0).astype(BF16)
        counts = dot((hot0 + hot1).astype(BF16), before)
        rank0 = jnp.sum(hot0 * counts, axis=0, keepdims=True)
        rank1 = jnp.sum(hot1 * counts, axis=0, keepdims=True)
        target0 = rank0 * experts + p0.astype(F32)
        target1 = rank1 * experts + p1.astype(F32)
        slot_ids = iota((slots, rows), 0).astype(F32)
        sel0 = slot_ids == target0
        sel1 = slot_ids == target1

        def emit(t, send):
            for s in range(cap):
                for c in range(hc):
                    scr[t, pl.ds(s * hc + c, experts, stride=cap * hc + 1), :] = send[
                        s * experts : (s + 1) * experts, c * LANE : (c + 1) * LANE
                    ]
            for e in range(experts):
                row = e * (cap * hc + 1)
                buf[t, e] = scr[t, row : row + cap * hc, :].astype(BF16)
            store = pltpu.make_async_copy(
                buf.at[t], out_hbm.at[:, pl.ds(t * cap * hc, cap * hc), :], sems.at[5 + t]
            )
            store.start()
            return store

        loads[2].wait()
        bnd[...] = dot_tn(pos_hot, bytes_ref[...]).astype(BF16)
        take = (jnp.where(sel0, 1.0, 0.0) + jnp.where(sel1, 1.0, 0.0)).astype(BF16)
        stores = [emit(0, dot(take, bnd[:, pl.ds(off, half)]))]
        loads[3].wait()
        logits = dot_nt(router_ref[...], bnd[...])
        l0 = jnp.sum(hot0 * logits, axis=0, keepdims=True)
        l1 = jnp.sum(hot1 * logits, axis=0, keepdims=True)
        mix0 = jax.nn.sigmoid(l0 - l1)
        mix1 = 1.0 - mix0
        low0 = mix0.astype(BF16).astype(F32)
        low1 = mix1.astype(BF16).astype(F32)
        take_mix = (jnp.where(sel0, low0, 0.0) + jnp.where(sel1, low1, 0.0)).astype(BF16)
        loads[4].wait()
        stores.append(emit(1, dot(take_mix, cot_ref[...])))
        meta_ref[...] = jnp.concatenate(
            [target0, target1, mix0, mix1, p0.astype(F32), p1.astype(F32), mix0, mix1], axis=0
        )
        for store in stores:
            store.wait()

    payload, meta = pl.pallas_call(
        dispatch_kernel,
        out_shape=(
            pltpu.HBM((experts, disp, LANE), BF16),
            pltpu.VMEM((8, rows), F32),
        ),
        in_specs=[aspec()] * 5,
        out_specs=(aspec(), vspec()),
        scratch_shapes=[
            pltpu.VMEM((byte_count, width), BF16),
            pltpu.VMEM((1, rows), jnp.int32),
            pltpu.VMEM((2, rows), jnp.int32),
            pltpu.VMEM((rows, half), BF16),
            pltpu.VMEM((experts, width), BF16),
            pltpu.VMEM((rows, width), BF16),
            pltpu.VMEM((2, experts * (cap * hc + 1), LANE), F32),
            pltpu.VMEM((2, experts, cap * hc, LANE), BF16),
            pltpu.SemaphoreType.DMA((7,)),
        ],
        compiler_params=params(),
        name="dispatch",
    )(
        hb(byte_states),
        hb(positions.reshape(1, rows)),
        hb(picks.T),
        hb(cotangent),
        hb(router_weight.T),
    )

    def exchange(x):
        return lax.all_to_all(x, "expert", split_axis=0, concat_axis=0, tiled=True)

    recv = exchange(payload).reshape(experts * disp, LANE)

    def aux_kernel(
        meta_ref, router_ref, hot_hbm, delta_hbm, mix_hbm, hot_ref, delta_ref, mix_ref, sems
    ):
        off = pl.multiple_of(pair_id() * half, half)
        slot_ids = iota((3 * LANE, rows), 0).astype(F32)
        for k in range(2):
            hot = jnp.where(slot_ids == meta_ref[k : k + 1, :], 1.0, 0.0)
            hot_ref[k * rows : (k + 1) * rows, :] = hot.T.astype(BF16)
        ids = iota((LANE, rows), 0).astype(F32)
        diff = jnp.where(ids == meta_ref[4:5, :], 1.0, 0.0) - jnp.where(
            ids == meta_ref[5:6, :], 1.0, 0.0
        )
        diff = diff.T.astype(BF16)[:, :experts]
        delta_ref[...] = dot(diff, router_ref[:, pl.ds(off, half)])
        cols = jnp.concatenate([meta_ref[...], jnp.zeros((LANE - 8, rows), F32)], axis=0)
        mix_ref[...] = cols.T
        copies = [
            pltpu.make_async_copy(hot_ref, hot_hbm, sems.at[0]),
            pltpu.make_async_copy(delta_ref, delta_hbm, sems.at[1]),
            pltpu.make_async_copy(mix_ref, mix_hbm, sems.at[2]),
        ]
        for copy in copies:
            copy.start()
        for copy in copies:
            copy.wait()

    hots, delta, mix_cols = pl.pallas_call(
        aux_kernel,
        out_shape=(
            pltpu.HBM((2 * rows, 3 * LANE), BF16),
            pltpu.HBM((rows, half), F32),
            pltpu.HBM((rows, LANE), F32),
        ),
        in_specs=[vspec()] * 2,
        out_specs=(aspec(),) * 3,
        scratch_shapes=[
            pltpu.VMEM((2 * rows, 3 * LANE), BF16),
            pltpu.VMEM((rows, half), F32),
            pltpu.VMEM((rows, LANE), F32),
            pltpu.SemaphoreType.DMA((3,)),
        ],
        compiler_params=params(),
        name="aux",
    )(vm(meta), router_weight.T)

    def stack_kernel(gate_hbm, up_hbm, down_hbm, low_ref, high_ref, sems):
        copies = []
        for i, src in enumerate((gate_hbm, up_hbm, down_hbm)):
            for j, dst in enumerate((low_ref, high_ref)):
                copies.append(
                    pltpu.make_async_copy(
                        src.at[0, pl.ds(j * part, part), :], dst.at[i], sems.at[2 * i + j]
                    )
                )
        for copy in copies:
            copy.start()
        for copy in copies:
            copy.wait()

    low, high = pl.pallas_call(
        stack_kernel,
        out_shape=(pltpu.VMEM((3, part, fh), BF16),) * 2,
        in_specs=[aspec()] * 3,
        out_specs=(vspec(),) * 2,
        scratch_shapes=[pltpu.SemaphoreType.DMA((6,))],
        compiler_params=params(),
        name="stack",
    )(hb(gate_weight), hb(up_weight), hb(down_weight))

    ahead = [(i, (i + 1) % dps) for i in range(dps)]
    behind = [(i, (i - 1) % dps) for i in range(dps)]
    low_prev = lax.ppermute(low, "dp", ahead)
    high_next = lax.ppermute(high, "dp", behind)
    high_prev = lax.ppermute(high, "dp", ahead)
    low_next = lax.ppermute(low, "dp", behind)
    low_far = lax.ppermute(low_prev, "dp", ahead)
    high_far = lax.ppermute(high_next, "dp", behind)
    pieces = (low, high, low_next, high_next, low_far, high_far, low_prev, high_prev)

    def assemble_kernel(*refs):
        out_hbm, sems = refs[2 * dps :]
        y = dp_id()
        copies = []
        for k in range(dps):
            for j in range(2):
                row = pl.multiple_of(((y + k) % dps) * shard + j * part, part)
                copies.append(
                    pltpu.make_async_copy(
                        refs[2 * k + j], out_hbm.at[:, pl.ds(row, part), :], sems.at[2 * k + j]
                    )
                )
        for copy in copies:
            copy.start()
        for copy in copies:
            copy.wait()

    full = pl.pallas_call(
        assemble_kernel,
        out_shape=pltpu.HBM((3, width, fh), BF16),
        in_specs=[vspec()] * (2 * dps),
        out_specs=aspec(),
        scratch_shapes=[pltpu.SemaphoreType.DMA((2 * dps,))],
        compiler_params=params(),
        name="assemble",
    )(*[vm(x) for x in pieces])

    swap = [(0, 1), (1, 0)]
    full_other = lax.ppermute(full, "pair", swap)
    recv_other = lax.ppermute(recv, "pair", swap)

    def unpack(ref, wide, x_dst, s_dst):
        for e in range(experts):
            wide[e * (disp + 1) : e * (disp + 1) + disp, :] = ref[
                e * disp : (e + 1) * disp, :
            ].astype(F32)
        for s in range(cap):
            for t, dst in ((0, x_dst), (1, s_dst)):
                for c in range(hc):
                    val = wide[pl.ds((t * cap + s) * hc + c, experts, stride=disp + 1), :]
                    dst[s * experts : (s + 1) * experts, c * LANE : (c + 1) * LANE] = val.astype(
                        BF16
                    )

    def fetch(own_hbm, oth_hbm, w_buf, sems, h):
        row = pl.multiple_of(h * half, half)
        return [
            pltpu.make_async_copy(
                src.at[:, pl.ds(row, half), :], w_buf.at[:, :, pl.ds(i * fh, fh)], sems.at[i]
            )
            for i, src in enumerate((own_hbm, oth_hbm))
        ]

    def own_kernel(recv_ref, own_hbm, oth_hbm, x_ref, pre_ref, w_buf, wide, s_buf, sems):
        loads = fetch(own_hbm, oth_hbm, w_buf, sems, pair_id())
        for load in loads:
            load.start()
        unpack(recv_ref, wide, x_ref, s_buf)
        for load in loads:
            load.wait()
        pre_ref[0] = dot(x_ref[...], w_buf[0])
        pre_ref[1] = dot(x_ref[...], w_buf[1])
        pre_ref[2] = dot(s_buf[...], w_buf[2])

    x_own, pre, w_own = pl.pallas_call(
        own_kernel,
        out_shape=(
            pltpu.VMEM((slots, half), BF16),
            pltpu.VMEM((3, slots, 2 * fh), F32),
            pltpu.VMEM((3, half, 2 * fh), BF16),
        ),
        in_specs=[vspec(), aspec(), aspec()],
        out_specs=(vspec(),) * 3,
        scratch_shapes=[
            pltpu.VMEM((experts * (disp + 1), LANE), F32),
            pltpu.VMEM((slots, half), BF16),
            pltpu.SemaphoreType.DMA((2,)),
        ],
        compiler_params=params(),
        name="own",
    )(vm(recv), hb(full), hb(full_other))

    def grads_kernel(
        recv_ref, own_hbm, oth_hbm, pre_ref, w_own_ref, x_ref, joined_ref, out_ref,
        wide, s_buf, w_buf, sems,
    ):
        loads = fetch(own_hbm, oth_hbm, w_buf, sems, 1 - pair_id())
        for load in loads:
            load.start()
        unpack(recv_ref, wide, x_ref, s_buf)
        for load in loads:
            load.wait()
        gate = pre_ref[0] + dot(x_ref[...], w_buf[0])
        up = pre_ref[1] + dot(x_ref[...], w_buf[1])
        grad = pre_ref[2] + dot(s_buf[...], w_buf[2])
        sigma = jax.nn.sigmoid(gate)
        activ = gate * sigma
        slope = sigma * (1.0 + gate * (1.0 - sigma))
        hidden = (activ * up).astype(BF16).astype(F32)
        mixed = jnp.sum(hidden * grad, axis=1, keepdims=True)
        gate_grad = (grad * up * slope).astype(BF16)
        up_grad = (grad * activ).astype(BF16)
        joined_ref[:, :fh] = gate_grad[:, :fh]
        joined_ref[:, fh:] = up_grad[:, :fh]
        pick = dot_nt(gate_grad, w_own_ref[0]) + dot_nt(up_grad, w_own_ref[1])
        for s in range(cap):
            total = pick[s * experts : (s + 1) * experts].reshape(experts, hc, LANE).astype(BF16)
            out_ref[:, s * hc // 2 : (s + 1) * hc // 2] = total.reshape(experts, hc // 2, 2, LANE)
        mixed = jnp.broadcast_to(mixed, (slots, LANE))
        high_mixed = mixed.astype(BF16).astype(F32)
        lane = iota((experts, LANE), 1)
        line = jnp.zeros((experts, LANE), F32)
        for s in range(cap):
            span = slice(s * experts, (s + 1) * experts)
            line = jnp.where(lane == s, high_mixed[span], line)
            line = jnp.where(lane == LANE // 2 + s, mixed[span] - high_mixed[span], line)
        line = jnp.stack([line, jnp.zeros((experts, LANE), F32)], axis=1)
        out_ref[:, back // 2 - 1 :] = line.reshape(experts, 1, 2, LANE).astype(BF16)

    x_other, joined, packed = pl.pallas_call(
        grads_kernel,
        out_shape=(
            pltpu.VMEM((slots, half), BF16),
            pltpu.VMEM((slots, 2 * fh), BF16),
            jax.ShapeDtypeStruct((experts, back // 2, 2, LANE), BF16),
        ),
        in_specs=[vspec(), aspec(), aspec(), vspec(), vspec()],
        out_specs=(vspec(),) * 3,
        scratch_shapes=[
            pltpu.VMEM((experts * (disp + 1), LANE), F32),
            pltpu.VMEM((slots, half), BF16),
            pltpu.VMEM((3, half, 2 * fh), BF16),
            pltpu.SemaphoreType.DMA((2,)),
        ],
        compiler_params=params(),
        name="grads",
    )(vm(recv_other), hb(full), hb(full_other), vm(pre), vm(w_own))

    def weight_kernel(own_ref, oth_ref, joined_ref, mine, next_low, next_high, far_low, far_high, prev_low, prev_high, x_all):
        p = pair_id()
        y = dp_id()
        x_all[:, pl.ds(pl.multiple_of(p * half, half), half)] = own_ref[...]
        x_all[:, pl.ds(pl.multiple_of((1 - p) * half, half), half)] = oth_ref[...]
        for k, dst in (
            (2, (far_low, far_high)),
            (1, (next_low, next_high)),
            (3, (prev_low, prev_high)),
            (0, (mine.at[:part], mine.at[part:])),
        ):
            col = pl.multiple_of(((y + k) % dps) * shard, shard)
            block = dot_tn(x_all[:, pl.ds(col, shard)], joined_ref[...]).astype(BF16)
            dst[0][...] = block[:part]
            dst[1][...] = block[part:]

    mine, next_low, next_high, far_low, far_high, prev_low, prev_high = pl.pallas_call(
        weight_kernel,
        out_shape=(pltpu.VMEM((shard, 2 * fh), BF16),)
        + (pltpu.VMEM((part, 2 * fh), BF16),) * 6,
        in_specs=[vspec()] * 3,
        out_specs=(vspec(),) * 7,
        scratch_shapes=[pltpu.VMEM((slots, width), BF16)],
        compiler_params=params(),
        name="weight",
    )(vm(x_own), vm(x_other), vm(joined))

    far_low = lax.ppermute(far_low, "dp", ahead)
    far_high = lax.ppermute(far_high, "dp", behind)
    got_high = lax.ppermute(next_high, "dp", ahead)
    got_low = lax.ppermute(prev_low, "dp", behind)

    def add_kernel(a_ref, b_ref, c_ref, d_ref, low_ref, high_ref):
        low_ref[...] = (a_ref[...].astype(F32) + b_ref[...].astype(F32)).astype(BF16)
        high_ref[...] = (c_ref[...].astype(F32) + d_ref[...].astype(F32)).astype(BF16)

    sum_low, sum_high = pl.pallas_call(
        add_kernel,
        out_shape=(pltpu.VMEM((part, 2 * fh), BF16),) * 2,
        in_specs=[vspec()] * 4,
        out_specs=(vspec(),) * 2,
        compiler_params=params(),
        name="add",
    )(vm(next_low), vm(far_low), vm(prev_high), vm(far_high))

    sum_low = lax.ppermute(sum_low, "dp", ahead)
    sum_high = lax.ppermute(sum_high, "dp", behind)

    returned = exchange(packed)

    def total_kernel(mine_ref, a_ref, b_ref, c_ref, d_ref, gate_ref, up_ref):
        for span, one, two in ((slice(0, part), a_ref, b_ref), (slice(part, shard), c_ref, d_ref)):
            total = mine_ref[span, :].astype(F32) + one[...].astype(F32) + two[...].astype(F32)
            total = total.astype(BF16)
            gate_ref[0, span, :] = total[:, :fh]
            up_ref[0, span, :] = total[:, fh:]

    gate_out, up_out = pl.pallas_call(
        total_kernel,
        out_shape=(jax.ShapeDtypeStruct((1, shard, fh), BF16),) * 2,
        in_specs=[vspec()] * 5,
        out_specs=(vspec(),) * 2,
        compiler_params=params(),
        name="total",
    )(*[vm(x) for x in (mine, sum_low, got_low, got_high, sum_high)])

    def combine_kernel(
        back_ref, hot_hbm, delta_hbm, mix_hbm, out_ref,
        grads, small, hot_ref, delta_ref, mix_ref, sems,
    ):
        loads = [
            pltpu.make_async_copy(hot_hbm, hot_ref, sems.at[0]),
            pltpu.make_async_copy(mix_hbm, mix_ref, sems.at[1]),
            pltpu.make_async_copy(delta_hbm, delta_ref, sems.at[2]),
        ]
        for load in loads:
            load.start()
        lane = jnp.bitwise_and(iota((experts, LANE), 1), LANE // 2 - 1)
        line = back_ref[:, back // 2 - 1 :].astype(F32).reshape(experts, 2 * LANE)[:, :LANE]
        for s in range(cap):
            span = slice(s * experts, (s + 1) * experts)
            block = back_ref[:, s * hc // 2 : (s + 1) * hc // 2].astype(F32)
            grads[span, :] = block.reshape(experts, half).astype(BF16)
            small[span, :] = jnp.where(lane == s, line, 0.0).astype(BF16)
        grads[slots:, :] = jnp.zeros((3 * LANE - slots, half), BF16)
        small[slots:, :] = jnp.zeros((3 * LANE - slots, LANE), BF16)
        for load in loads:
            load.wait()
        hot0 = hot_ref[:rows, :]
        hot1 = hot_ref[rows:, :]
        u0 = jnp.sum(dot(hot0, small[...]), axis=1, keepdims=True)
        u1 = jnp.sum(dot(hot1, small[...]), axis=1, keepdims=True)
        logit = mix_ref[:, 3:4] * u0 - mix_ref[:, 2:3] * u1
        out_ref[...] = (dot(hot0 + hot1, grads[...]) + logit * delta_ref[...]).astype(BF16)

    row_half = pl.pallas_call(
        combine_kernel,
        out_shape=pltpu.VMEM((rows, half), BF16),
        in_specs=[vspec()] + [aspec()] * 3,
        out_specs=vspec(),
        scratch_shapes=[
            pltpu.VMEM((3 * LANE, half), BF16),
            pltpu.VMEM((3 * LANE, LANE), BF16),
            pltpu.VMEM((2 * rows, 3 * LANE), BF16),
            pltpu.VMEM((rows, half), F32),
            pltpu.VMEM((rows, LANE), F32),
            pltpu.SemaphoreType.DMA((3,)),
        ],
        compiler_params=params(),
        name="combine",
    )(vm(returned), hb(hots), hb(delta), hb(mix_cols))

    row_half_other = lax.ppermute(row_half, "pair", swap)

    def join_kernel(own_ref, oth_ref, out_hbm, sems):
        p = pair_id()
        copies = [
            pltpu.make_async_copy(
                src, out_hbm.at[:, pl.ds(pl.multiple_of(h * half, half), half)], sems.at[i]
            )
            for i, (src, h) in enumerate(((own_ref, p), (oth_ref, 1 - p)))
        ]
        for copy in copies:
            copy.start()
        for copy in copies:
            copy.wait()

    row_grad = pl.pallas_call(
        join_kernel,
        out_shape=jax.ShapeDtypeStruct((rows, width), BF16),
        in_specs=[vspec()] * 2,
        out_specs=aspec(),
        scratch_shapes=[pltpu.SemaphoreType.DMA((2,))],
        compiler_params=params(),
        name="join",
    )(vm(row_half), vm(row_half_other))
    return (row_grad, gate_out, up_out)


def solution(mesh):
    in_specs = (
        P(("expert", "dp"), None),
        P(("expert", "dp")),
        P(("expert", "dp"), None),
        P(("expert", "dp"), None),
        P(),
        P("expert", "dp", "pair"),
        P("expert", "dp", "pair"),
        P("expert", "dp", "pair"),
    )
    out_specs = (P(("expert", "dp"), None), P("expert", "dp", "pair"), P("expert", "dp", "pair"))

    return jax.shard_map(local, mesh=mesh, in_specs=in_specs, out_specs=out_specs, check_vma=False)
```

```python
import jax
import jax.numpy as jnp
from jax import lax
from jax.experimental import pallas as pl
from jax.experimental.pallas import tpu as pltpu
from jax.sharding import PartitionSpec as P


F32 = jnp.float32
BF16 = jnp.bfloat16
LANE = 128
VMEM_LIMIT = 32 * 1024 * 1024


def vm(x):
    return pltpu.with_memory_space_constraint(x, pltpu.VMEM)


def hb(x):
    return pltpu.with_memory_space_constraint(x, pltpu.HBM)


def vspec():
    return pl.BlockSpec(memory_space=pltpu.VMEM)


def aspec():
    return pl.BlockSpec(memory_space=pl.ANY)


def pair_id():
    return lax.axis_index("pair").astype(jnp.int32)


def dp_id():
    return lax.axis_index("dp").astype(jnp.int32)


def params():
    return pltpu.CompilerParams(vmem_limit_bytes=VMEM_LIMIT)


def iota(shape, dim):
    return lax.broadcasted_iota(jnp.int32, shape, dim)


def dot(a, b):
    return jnp.dot(a, b, preferred_element_type=F32)


def dot_nt(a, b):
    return lax.dot_general(a, b, (((1,), (1,)), ((), ())), preferred_element_type=F32)


def dot_tn(a, b):
    return lax.dot_general(a, b, (((0,), (0,)), ((), ())), preferred_element_type=F32)


def local(
    byte_states, positions, picks, cotangent, router_weight, gate_weight, up_weight, down_weight
):
    byte_count, width = byte_states.shape
    rows = positions.shape[0]
    experts = router_weight.shape[1]
    cap = 5
    slots = cap * experts
    half = width // 2
    hc = half // LANE
    shard, fh = gate_weight.shape[1], gate_weight.shape[2]
    dps = width // shard
    disp = cap * 2 * hc
    back = cap * hc + 2
    part = shard // 2

    def dispatch_kernel(
        bytes_hbm, pos_hbm, picks_hbm, cot_hbm, router_hbm, out_hbm, meta_ref,
        bytes_ref, pos_ref, picks_ref, cot_ref, router_ref, bnd, scr, buf, sems,
    ):
        off = pl.multiple_of(pair_id() * half, half)
        loads = [
            pltpu.make_async_copy(pos_hbm, pos_ref, sems.at[0]),
            pltpu.make_async_copy(picks_hbm, picks_ref, sems.at[1]),
            pltpu.make_async_copy(bytes_hbm, bytes_ref, sems.at[2]),
            pltpu.make_async_copy(router_hbm, router_ref, sems.at[3]),
            pltpu.make_async_copy(cot_hbm.at[:, pl.ds(off, half)], cot_ref, sems.at[4]),
        ]
        for load in loads:
            load.start()
        loads[0].wait()
        loads[1].wait()
        pos = jnp.bitwise_and(pos_ref[...], byte_count - 1)
        pos_hot = jnp.where(iota((byte_count, rows), 0) == pos, 1.0, 0.0).astype(BF16)
        p0 = picks_ref[0:1, :]
        p1 = picks_ref[1:2, :]
        ids = iota((experts, rows), 0)
        hot0 = jnp.where(ids == p0, 1.0, 0.0)
        hot1 = jnp.where(ids == p1, 1.0, 0.0)
        before = jnp.where(iota((rows, rows), 0) < iota((rows, rows), 1), 1.0, 0.0).astype(BF16)
        counts = dot((hot0 + hot1).astype(BF16), before)
        rank0 = jnp.sum(hot0 * counts, axis=0, keepdims=True)
        rank1 = jnp.sum(hot1 * counts, axis=0, keepdims=True)
        target0 = rank0 * experts + p0.astype(F32)
        target1 = rank1 * experts + p1.astype(F32)
        slot_ids = iota((slots, rows), 0).astype(F32)
        sel0 = slot_ids == target0
        sel1 = slot_ids == target1

        def emit(t, send):
            for s in range(cap):
                for c in range(hc):
                    scr[t, pl.ds(s * hc + c, experts, stride=cap * hc + 1), :] = send[
                        s * experts : (s + 1) * experts, c * LANE : (c + 1) * LANE
                    ]
            for e in range(experts):
                row = e * (cap * hc + 1)
                buf[t, e] = scr[t, row : row + cap * hc, :].astype(BF16)
            store = pltpu.make_async_copy(
                buf.at[t], out_hbm.at[:, pl.ds(t * cap * hc, cap * hc), :], sems.at[5 + t]
            )
            store.start()
            return store

        loads[2].wait()
        bnd[...] = dot_tn(pos_hot, bytes_ref[...]).astype(BF16)
        take = (jnp.where(sel0, 1.0, 0.0) + jnp.where(sel1, 1.0, 0.0)).astype(BF16)
        stores = [emit(0, dot(take, bnd[:, pl.ds(off, half)]))]
        loads[3].wait()
        logits = dot_nt(router_ref[...], bnd[...])
        l0 = jnp.sum(hot0 * logits, axis=0, keepdims=True)
        l1 = jnp.sum(hot1 * logits, axis=0, keepdims=True)
        mix0 = jax.nn.sigmoid(l0 - l1)
        mix1 = 1.0 - mix0
        low0 = mix0.astype(BF16).astype(F32)
        low1 = mix1.astype(BF16).astype(F32)
        take_mix = (jnp.where(sel0, low0, 0.0) + jnp.where(sel1, low1, 0.0)).astype(BF16)
        loads[4].wait()
        stores.append(emit(1, dot(take_mix, cot_ref[...])))
        meta_ref[...] = jnp.concatenate(
            [target0, target1, mix0, mix1, p0.astype(F32), p1.astype(F32), mix0, mix1], axis=0
        )
        for store in stores:
            store.wait()

    payload, meta = pl.pallas_call(
        dispatch_kernel,
        out_shape=(
            pltpu.HBM((experts, disp, LANE), BF16),
            pltpu.VMEM((8, rows), F32),
        ),
        in_specs=[aspec()] * 5,
        out_specs=(aspec(), vspec()),
        scratch_shapes=[
            pltpu.VMEM((byte_count, width), BF16),
            pltpu.VMEM((1, rows), jnp.int32),
            pltpu.VMEM((2, rows), jnp.int32),
            pltpu.VMEM((rows, half), BF16),
            pltpu.VMEM((experts, width), BF16),
            pltpu.VMEM((rows, width), BF16),
            pltpu.VMEM((2, experts * (cap * hc + 1), LANE), F32),
            pltpu.VMEM((2, experts, cap * hc, LANE), BF16),
            pltpu.SemaphoreType.DMA((7,)),
        ],
        compiler_params=params(),
        name="dispatch",
    )(
        hb(byte_states),
        hb(positions.reshape(1, rows)),
        hb(picks.T),
        hb(cotangent),
        hb(router_weight.T),
    )

    def exchange(x):
        return lax.all_to_all(x, "expert", split_axis=0, concat_axis=0, tiled=True)

    recv = exchange(payload).reshape(experts * disp, LANE)

    def aux_kernel(
        meta_ref, router_ref, hot_hbm, delta_hbm, mix_hbm, hot_ref, delta_ref, mix_ref, sems
    ):
        off = pl.multiple_of(pair_id() * half, half)
        slot_ids = iota((3 * LANE, rows), 0).astype(F32)
        for k in range(2):
            hot = jnp.where(slot_ids == meta_ref[k : k + 1, :], 1.0, 0.0)
            hot_ref[k * rows : (k + 1) * rows, :] = hot.T.astype(BF16)
        ids = iota((LANE, rows), 0).astype(F32)
        diff = jnp.where(ids == meta_ref[4:5, :], 1.0, 0.0) - jnp.where(
            ids == meta_ref[5:6, :], 1.0, 0.0
        )
        diff = diff.T.astype(BF16)[:, :experts]
        delta_ref[...] = dot(diff, router_ref[:, pl.ds(off, half)])
        cols = jnp.concatenate([meta_ref[...], jnp.zeros((LANE - 8, rows), F32)], axis=0)
        mix_ref[...] = cols.T
        copies = [
            pltpu.make_async_copy(hot_ref, hot_hbm, sems.at[0]),
            pltpu.make_async_copy(delta_ref, delta_hbm, sems.at[1]),
            pltpu.make_async_copy(mix_ref, mix_hbm, sems.at[2]),
        ]
        for copy in copies:
            copy.start()
        for copy in copies:
            copy.wait()

    hots, delta, mix_cols = pl.pallas_call(
        aux_kernel,
        out_shape=(
            pltpu.HBM((2 * rows, 3 * LANE), BF16),
            pltpu.HBM((rows, half), F32),
            pltpu.HBM((rows, LANE), F32),
        ),
        in_specs=[vspec()] * 2,
        out_specs=(aspec(),) * 3,
        scratch_shapes=[
            pltpu.VMEM((2 * rows, 3 * LANE), BF16),
            pltpu.VMEM((rows, half), F32),
            pltpu.VMEM((rows, LANE), F32),
            pltpu.SemaphoreType.DMA((3,)),
        ],
        compiler_params=params(),
        name="aux",
    )(vm(meta), router_weight.T)

    def stack_kernel(gate_hbm, up_hbm, down_hbm, low_ref, high_ref, sems):
        copies = []
        for i, src in enumerate((gate_hbm, up_hbm, down_hbm)):
            for j, dst in enumerate((low_ref, high_ref)):
                copies.append(
                    pltpu.make_async_copy(
                        src.at[0, pl.ds(j * part, part), :], dst.at[i], sems.at[2 * i + j]
                    )
                )
        for copy in copies:
            copy.start()
        for copy in copies:
            copy.wait()

    low, high = pl.pallas_call(
        stack_kernel,
        out_shape=(pltpu.VMEM((3, part, fh), BF16),) * 2,
        in_specs=[aspec()] * 3,
        out_specs=(vspec(),) * 2,
        scratch_shapes=[pltpu.SemaphoreType.DMA((6,))],
        compiler_params=params(),
        name="stack",
    )(hb(gate_weight), hb(up_weight), hb(down_weight))

    ahead = [(i, (i + 1) % dps) for i in range(dps)]
    behind = [(i, (i - 1) % dps) for i in range(dps)]
    low_prev = lax.ppermute(low, "dp", ahead)
    high_next = lax.ppermute(high, "dp", behind)
    high_prev = lax.ppermute(high, "dp", ahead)
    low_next = lax.ppermute(low, "dp", behind)
    low_far = lax.ppermute(low_prev, "dp", ahead)
    high_far = lax.ppermute(high_next, "dp", behind)
    pieces = (low, high, low_next, high_next, low_far, high_far, low_prev, high_prev)

    def assemble_kernel(*refs):
        out_hbm, sems = refs[2 * dps :]
        y = dp_id()
        copies = []
        for k in range(dps):
            for j in range(2):
                row = pl.multiple_of(((y + k) % dps) * shard + j * part, part)
                copies.append(
                    pltpu.make_async_copy(
                        refs[2 * k + j], out_hbm.at[:, pl.ds(row, part), :], sems.at[2 * k + j]
                    )
                )
        for copy in copies:
            copy.start()
        for copy in copies:
            copy.wait()

    full = pl.pallas_call(
        assemble_kernel,
        out_shape=pltpu.HBM((3, width, fh), BF16),
        in_specs=[vspec()] * (2 * dps),
        out_specs=aspec(),
        scratch_shapes=[pltpu.SemaphoreType.DMA((2 * dps,))],
        compiler_params=params(),
        name="assemble",
    )(*[vm(x) for x in pieces])

    swap = [(0, 1), (1, 0)]
    full_other = lax.ppermute(full, "pair", swap)
    recv_other = lax.ppermute(recv, "pair", swap)

    def unpack(ref, wide, x_dst, s_dst):
        for e in range(experts):
            wide[e * (disp + 1) : e * (disp + 1) + disp, :] = ref[
                e * disp : (e + 1) * disp, :
            ].astype(F32)
        for s in range(cap):
            for t, dst in ((0, x_dst), (1, s_dst)):
                for c in range(hc):
                    val = wide[pl.ds((t * cap + s) * hc + c, experts, stride=disp + 1), :]
                    dst[s * experts : (s + 1) * experts, c * LANE : (c + 1) * LANE] = val.astype(
                        BF16
                    )

    def fetch(own_hbm, oth_hbm, w_buf, sems, h):
        row = pl.multiple_of(h * half, half)
        loads = [
            [
                pltpu.make_async_copy(
                    src.at[k, pl.ds(row, half), :], w_buf.at[k, :, pl.ds(i * fh, fh)], sems.at[k, i]
                )
                for i, src in enumerate((own_hbm, oth_hbm))
            ]
            for k in range(3)
        ]
        for two in loads:
            for load in two:
                load.start()
        return loads

    def project(loads, k, x, w_buf):
        for load in loads[k]:
            load.wait()
        return dot(x, w_buf[k])

    def own_kernel(recv_ref, own_hbm, oth_hbm, x_ref, pre_ref, w_buf, wide, s_buf, sems):
        loads = fetch(own_hbm, oth_hbm, w_buf, sems, pair_id())
        unpack(recv_ref, wide, x_ref, s_buf)
        pre_ref[0] = project(loads, 0, x_ref[...], w_buf)
        pre_ref[1] = project(loads, 1, x_ref[...], w_buf)
        pre_ref[2] = project(loads, 2, s_buf[...], w_buf)

    x_own, pre, w_own = pl.pallas_call(
        own_kernel,
        out_shape=(
            pltpu.VMEM((slots, half), BF16),
            pltpu.VMEM((3, slots, 2 * fh), F32),
            pltpu.VMEM((3, half, 2 * fh), BF16),
        ),
        in_specs=[vspec(), aspec(), aspec()],
        out_specs=(vspec(),) * 3,
        scratch_shapes=[
            pltpu.VMEM((experts * (disp + 1), LANE), F32),
            pltpu.VMEM((slots, half), BF16),
            pltpu.SemaphoreType.DMA((3, 2)),
        ],
        compiler_params=params(),
        name="own",
    )(vm(recv), hb(full), hb(full_other))

    def grads_kernel(
        recv_ref, own_hbm, oth_hbm, pre_ref, w_own_ref, x_ref, joined_ref, out_ref,
        wide, s_buf, w_buf, sems,
    ):
        loads = fetch(own_hbm, oth_hbm, w_buf, sems, 1 - pair_id())
        unpack(recv_ref, wide, x_ref, s_buf)
        gate = pre_ref[0] + project(loads, 0, x_ref[...], w_buf)
        up = pre_ref[1] + project(loads, 1, x_ref[...], w_buf)
        grad = pre_ref[2] + project(loads, 2, s_buf[...], w_buf)
        sigma = jax.nn.sigmoid(gate)
        activ = gate * sigma
        slope = sigma * (1.0 + gate * (1.0 - sigma))
        hidden = (activ * up).astype(BF16).astype(F32)
        mixed = jnp.sum(hidden * grad, axis=1, keepdims=True)
        gate_grad = (grad * up * slope).astype(BF16)
        up_grad = (grad * activ).astype(BF16)
        joined_ref[:, :fh] = gate_grad[:, :fh]
        joined_ref[:, fh:] = up_grad[:, :fh]
        pick = dot_nt(gate_grad, w_own_ref[0]) + dot_nt(up_grad, w_own_ref[1])
        for s in range(cap):
            total = pick[s * experts : (s + 1) * experts].reshape(experts, hc, LANE).astype(BF16)
            out_ref[:, s * hc // 2 : (s + 1) * hc // 2] = total.reshape(experts, hc // 2, 2, LANE)
        mixed = jnp.broadcast_to(mixed, (slots, LANE))
        high_mixed = mixed.astype(BF16).astype(F32)
        lane = iota((experts, LANE), 1)
        line = jnp.zeros((experts, LANE), F32)
        for s in range(cap):
            span = slice(s * experts, (s + 1) * experts)
            line = jnp.where(lane == s, high_mixed[span], line)
            line = jnp.where(lane == LANE // 2 + s, mixed[span] - high_mixed[span], line)
        line = jnp.stack([line, jnp.zeros((experts, LANE), F32)], axis=1)
        out_ref[:, back // 2 - 1 :] = line.reshape(experts, 1, 2, LANE).astype(BF16)

    x_other, joined, packed = pl.pallas_call(
        grads_kernel,
        out_shape=(
            pltpu.VMEM((slots, half), BF16),
            pltpu.VMEM((slots, 2 * fh), BF16),
            jax.ShapeDtypeStruct((experts, back // 2, 2, LANE), BF16),
        ),
        in_specs=[vspec(), aspec(), aspec(), vspec(), vspec()],
        out_specs=(vspec(),) * 3,
        scratch_shapes=[
            pltpu.VMEM((experts * (disp + 1), LANE), F32),
            pltpu.VMEM((slots, half), BF16),
            pltpu.VMEM((3, half, 2 * fh), BF16),
            pltpu.SemaphoreType.DMA((3, 2)),
        ],
        compiler_params=params(),
        name="grads",
    )(vm(recv_other), hb(full), hb(full_other), vm(pre), vm(w_own))

    def weight_kernel(own_ref, oth_ref, joined_ref, mine, next_low, next_high, far_low, far_high, prev_low, prev_high, x_all):
        p = pair_id()
        y = dp_id()
        x_all[:, pl.ds(pl.multiple_of(p * half, half), half)] = own_ref[...]
        x_all[:, pl.ds(pl.multiple_of((1 - p) * half, half), half)] = oth_ref[...]
        for k, dst in (
            (2, (far_low, far_high)),
            (1, (next_low, next_high)),
            (3, (prev_low, prev_high)),
            (0, (mine.at[:part], mine.at[part:])),
        ):
            col = pl.multiple_of(((y + k) % dps) * shard, shard)
            block = dot_tn(x_all[:, pl.ds(col, shard)], joined_ref[...]).astype(BF16)
            dst[0][...] = block[:part]
            dst[1][...] = block[part:]

    mine, next_low, next_high, far_low, far_high, prev_low, prev_high = pl.pallas_call(
        weight_kernel,
        out_shape=(pltpu.VMEM((shard, 2 * fh), BF16),)
        + (pltpu.VMEM((part, 2 * fh), BF16),) * 6,
        in_specs=[vspec()] * 3,
        out_specs=(vspec(),) * 7,
        scratch_shapes=[pltpu.VMEM((slots, width), BF16)],
        compiler_params=params(),
        name="weight",
    )(vm(x_own), vm(x_other), vm(joined))

    far_low = lax.ppermute(far_low, "dp", ahead)
    far_high = lax.ppermute(far_high, "dp", behind)
    got_high = lax.ppermute(next_high, "dp", ahead)
    got_low = lax.ppermute(prev_low, "dp", behind)

    def add_kernel(a_ref, b_ref, c_ref, d_ref, low_ref, high_ref):
        low_ref[...] = (a_ref[...].astype(F32) + b_ref[...].astype(F32)).astype(BF16)
        high_ref[...] = (c_ref[...].astype(F32) + d_ref[...].astype(F32)).astype(BF16)

    sum_low, sum_high = pl.pallas_call(
        add_kernel,
        out_shape=(pltpu.VMEM((part, 2 * fh), BF16),) * 2,
        in_specs=[vspec()] * 4,
        out_specs=(vspec(),) * 2,
        compiler_params=params(),
        name="add",
    )(vm(next_low), vm(far_low), vm(prev_high), vm(far_high))

    sum_low = lax.ppermute(sum_low, "dp", ahead)
    sum_high = lax.ppermute(sum_high, "dp", behind)

    returned = exchange(packed)

    def total_kernel(mine_ref, a_ref, b_ref, c_ref, d_ref, gate_ref, up_ref):
        for span, one, two in ((slice(0, part), a_ref, b_ref), (slice(part, shard), c_ref, d_ref)):
            total = mine_ref[span, :].astype(F32) + one[...].astype(F32) + two[...].astype(F32)
            total = total.astype(BF16)
            gate_ref[0, span, :] = total[:, :fh]
            up_ref[0, span, :] = total[:, fh:]

    gate_out, up_out = pl.pallas_call(
        total_kernel,
        out_shape=(jax.ShapeDtypeStruct((1, shard, fh), BF16),) * 2,
        in_specs=[vspec()] * 5,
        out_specs=(vspec(),) * 2,
        compiler_params=params(),
        name="total",
    )(*[vm(x) for x in (mine, sum_low, got_low, got_high, sum_high)])

    def combine_kernel(
        back_ref, hot_hbm, delta_hbm, mix_hbm, out_ref,
        grads, small, hot_ref, delta_ref, mix_ref, sems,
    ):
        loads = [
            pltpu.make_async_copy(hot_hbm, hot_ref, sems.at[0]),
            pltpu.make_async_copy(mix_hbm, mix_ref, sems.at[1]),
            pltpu.make_async_copy(delta_hbm, delta_ref, sems.at[2]),
        ]
        for load in loads:
            load.start()
        lane = jnp.bitwise_and(iota((experts, LANE), 1), LANE // 2 - 1)
        line = back_ref[:, back // 2 - 1 :].astype(F32).reshape(experts, 2 * LANE)[:, :LANE]
        for s in range(cap):
            span = slice(s * experts, (s + 1) * experts)
            block = back_ref[:, s * hc // 2 : (s + 1) * hc // 2].astype(F32)
            grads[span, :] = block.reshape(experts, half).astype(BF16)
            small[span, :] = jnp.where(lane == s, line, 0.0).astype(BF16)
        grads[slots:, :] = jnp.zeros((3 * LANE - slots, half), BF16)
        small[slots:, :] = jnp.zeros((3 * LANE - slots, LANE), BF16)
        for load in loads:
            load.wait()
        hot0 = hot_ref[:rows, :]
        hot1 = hot_ref[rows:, :]
        u0 = jnp.sum(dot(hot0, small[...]), axis=1, keepdims=True)
        u1 = jnp.sum(dot(hot1, small[...]), axis=1, keepdims=True)
        logit = mix_ref[:, 3:4] * u0 - mix_ref[:, 2:3] * u1
        out_ref[...] = (dot(hot0 + hot1, grads[...]) + logit * delta_ref[...]).astype(BF16)

    row_half = pl.pallas_call(
        combine_kernel,
        out_shape=pltpu.VMEM((rows, half), BF16),
        in_specs=[vspec()] + [aspec()] * 3,
        out_specs=vspec(),
        scratch_shapes=[
            pltpu.VMEM((3 * LANE, half), BF16),
            pltpu.VMEM((3 * LANE, LANE), BF16),
            pltpu.VMEM((2 * rows, 3 * LANE), BF16),
            pltpu.VMEM((rows, half), F32),
            pltpu.VMEM((rows, LANE), F32),
            pltpu.SemaphoreType.DMA((3,)),
        ],
        compiler_params=params(),
        name="combine",
    )(vm(returned), hb(hots), hb(delta), hb(mix_cols))

    row_half_other = lax.ppermute(row_half, "pair", swap)

    def join_kernel(own_ref, oth_ref, out_hbm, sems):
        p = pair_id()
        copies = [
            pltpu.make_async_copy(
                src, out_hbm.at[:, pl.ds(pl.multiple_of(h * half, half), half)], sems.at[i]
            )
            for i, (src, h) in enumerate(((own_ref, p), (oth_ref, 1 - p)))
        ]
        for copy in copies:
            copy.start()
        for copy in copies:
            copy.wait()

    row_grad = pl.pallas_call(
        join_kernel,
        out_shape=jax.ShapeDtypeStruct((rows, width), BF16),
        in_specs=[vspec()] * 2,
        out_specs=aspec(),
        scratch_shapes=[pltpu.SemaphoreType.DMA((2,))],
        compiler_params=params(),
        name="join",
    )(vm(row_half), vm(row_half_other))
    return (row_grad, gate_out, up_out)


def solution(mesh):
    in_specs = (
        P(("expert", "dp"), None),
        P(("expert", "dp")),
        P(("expert", "dp"), None),
        P(("expert", "dp"), None),
        P(),
        P("expert", "dp", "pair"),
        P("expert", "dp", "pair"),
        P("expert", "dp", "pair"),
    )
    out_specs = (P(("expert", "dp"), None), P("expert", "dp", "pair"), P("expert", "dp", "pair"))

    return jax.shard_map(local, mesh=mesh, in_specs=in_specs, out_specs=out_specs, check_vma=False)
```
